32 devices in a mesh: tm: 4 (over x, core), space: 8 (over z, y).
Axes of the slice: x: 2, y: 2, z: 4, core: 2. Of those that a mesh axis runs over, the one named last changes fastest.
Arguments:
- volume: float32 [4, 128, 8, 2048], P('tm', 'space'), may hold values from -6 to 6
- warp_coef: float32 [4, 4, 4, 128, 2048], P('tm', None, None, 'space'), may hold values from 0.05 to 0.4
- offsets: int32 [4, 8, 4], P('tm', 'space'), may hold values from -6 to 6
- thresholds: float32 [4], replicated, may hold values from 0.1 to 0.5
Outputs:
- regularized: float32 [4, 128, 8, 2048], P('tm', 'space')
The draws below stay inside these ranges and needn't reach their ends.
All inputs are finite; a program needn't handle non-finite values.
Results may differ from the reference program's by a relative error of at most 0.00002.
Values sent between devices are 32-bit elements; how exact they have to be, the bound alone decides.
No kernel may reach another device: no remote copies, remote signals or barrier semaphores. Data moves between devices by JAX's collectives and lax.ppermute only.
A program may use at most 64 MiB of HBM per device.

```python
import jax
import jax.numpy as jnp
import numpy as np
from jax import lax

X = 2048
YW = 8
Z_DEV = 16
BAND = 4
SECTIONS = 4
SWEEPS = 4
FRAMES = 4
NZ = 128
N_TM = 4
N_SPACE = 8


def set_ends(values, own_key, low, largest):
    longest = values.shape.index(max(values.shape))
    spots = []
    for shift in (0, 1):
        where = [jax.random.randint(jax.random.fold_in(own_key, axis), (), 0, length) for axis, length in enumerate(values.shape)]
        where[longest] = (where[longest] + shift) % values.shape[longest]
        spots.append(tuple(where))
    return values.at[spots[0]].set(low).at[spots[1]].set(largest)


def level_of(rng, shape, split, low, high):
    def one(axis_at, shards_of):
        steps = jax.random.uniform(jax.random.fold_in(jax.random.fold_in(rng, 6), axis_at), (shards_of,), jnp.float32, low / len(split), high / len(split))
        return jnp.repeat(jnp.exp(steps), shape[axis_at] // shards_of).reshape((-1,) + (1,) * (len(shape) - axis_at - 1))

    gain = one(*split[0])
    for cut in split[1:]:
        gain = gain * one(*cut)
    return gain


def centred(own_key, extent, deviation, most, split=(), held_as=jnp.bfloat16):
    values = deviation * jax.random.normal(own_key, extent, jnp.float32)
    if split:
        values = values * level_of(own_key, extent, split, -0.22, 0.18)
    return jnp.clip(values, -most, most).astype(held_as)


def setup_inputs(seed: int = 0) -> dict:
    keys = jax.random.split(jax.random.key(seed), 5)
    return {
        "volume": centred(keys[0], (FRAMES, NZ, YW, X), 1.0, 6.0, ((0, 4), (1, 8)), jnp.float32),
        "warp_coef": jnp.clip(0.05 + 0.35 * jax.random.uniform(keys[1], (FRAMES, SECTIONS, BAND, NZ, X), jnp.float32) ** level_of(keys[1], (FRAMES, SECTIONS, BAND, NZ, X), ((0, 4), (3, 8)), -0.2, 0.2), 0.05, 0.4),
        "offsets": set_ends(jax.random.randint(keys[2], (FRAMES, N_SPACE, SECTIONS), -6, 7), jax.random.fold_in(keys[2], 1), -6, 6).astype(jnp.int32),
        "thresholds": jnp.clip(jax.random.uniform(keys[3], (SECTIONS,), jnp.float32, 0.1, 0.5), 0.1, 0.5),
    }


margin_cells = 10
depth_rate = 0.4
plane_rate = 0.05
root_half = 0.7071067811865476


def edge_flux(change, weight):
    return weight * change / (1.0 + change * change * 0.25)


def spread(fluxes, dim_index):
    after = [(0, 0)] * fluxes.ndim
    before = [(0, 0)] * fluxes.ndim
    after[dim_index] = (0, 1)
    before[dim_index] = (1, 0)
    return jnp.pad(fluxes, after) - jnp.pad(fluxes, before)


def diffuse_once(field):
    result = field
    for dim_index, weight in ((1, depth_rate), (2, plane_rate), (3, plane_rate)):
        result = result + spread(edge_flux(jnp.diff(field, axis=dim_index), weight), dim_index)
    return result


def take_rows(block, start):
    return lax.dynamic_slice_in_dim(block, start, X, 2)


def warp_frames(field, coeffs, offset_table):
    padded = jnp.pad(field, ((0, 0), (0, 0), (0, 0), (margin_cells, margin_cells)))
    pieces = []
    for slab_index in range(N_SPACE):
        first_plane = slab_index * Z_DEV
        slab_block = padded[:, first_plane:first_plane + Z_DEV]
        total = jnp.zeros((field.shape[0], Z_DEV, YW, X), jnp.float32)
        for band_index in range(BAND):
            starts = (margin_cells + offset_table[:, slab_index] + band_index - BAND // 2).astype(jnp.int32)
            shifted = jax.vmap(take_rows)(slab_block, starts)
            total = total + coeffs[:, band_index, first_plane:first_plane + Z_DEV][:, :, None, :] * shifted
        pieces.append(total)
    return jnp.concatenate(pieces, axis=1)


def reference(volume, warp_coef, offsets, thresholds):
    levels = int(N_TM).bit_length() - 1
    current = volume
    frame_ids = np.arange(FRAMES)
    for step_index in range(SECTIONS):
        bit_index = step_index % levels
        partner = current[frame_ids ^ (1 << bit_index)]
        warped = warp_frames(partner, warp_coef[:, step_index], offsets[:, :, step_index])
        is_lower = jnp.asarray(((frame_ids >> bit_index) & 1) == 0)[:, None, None, None]
        upper_value = (current - warped) * root_half
        level = thresholds[step_index]
        shrunk = upper_value - jnp.clip(upper_value, -level, level)
        current = jnp.where(is_lower, (current + warped) * root_half, shrunk)
        for sweep_index in range(SWEEPS):
            current = diffuse_once(current)
    return current
```

```python
import functools

import jax
import jax.numpy as jnp
from jax import lax
from jax.experimental import pallas as pl
from jax.experimental.pallas import tpu as pltpu
from jax.sharding import PartitionSpec as P

BAND = 4
SECTIONS = 4
SWEEPS = 4
REACH = 6

depth_rate = 0.4
plane_rate = 0.05
root_half = 0.7071067811865476

LANES = 128
SPARE = 64
EDGE = SWEEPS
GROUP = 6
VMEM = pltpu.VMEM
SMEM = pltpu.SMEM


def cells(value):
    return [value[:, i : i + LANES] for i in range(0, value.shape[1], LANES)]


def joined(parts):
    return jnp.concatenate(parts, axis=1)


def lane_ids():
    return lax.broadcasted_iota(jnp.int32, (8, LANES), 1)


def quotient(change):
    return change / (1.0 + change * change)


def moved_right(parts, amount, first):
    turned = [pltpu.roll(part, amount, 1) for part in parts]
    own = lane_ids() >= amount
    ahead = [first] + turned[:-1]
    return [jnp.where(own, a, b) for a, b in zip(turned, ahead)]


def moved_left(parts, amount):
    turned = [pltpu.roll(part, (LANES - amount) % LANES, 1) for part in parts]
    own = lane_ids() < LANES - amount
    return [jnp.where(own, a, b) for a, b in zip(turned, turned[1:])]


def warped_plane(field, coeff_rows, offset):
    zero = jnp.zeros((8, LANES), jnp.float32)
    behind = moved_right(cells(field) + [zero], REACH + BAND // 2, zero)
    total = None
    for band_index in range(BAND):
        shifted = joined(moved_left(behind, offset + REACH + band_index))
        term = jnp.broadcast_to(coeff_rows[band_index], shifted.shape) * shifted
        total = term if total is None else total + term
    return total


def haar(own, warped, sign, level, scale):
    value = (own + sign * warped) * scale
    return value - jnp.clip(value, -level, level)


class Sweep:
    def __init__(self, width, edge_first, edge_last, last_lane):
        rows = lax.broadcasted_iota(jnp.int32, (8, width), 0)
        self.inner_rows = rows < 7
        lanes = lane_ids()
        self.first = jnp.where(lanes == SPARE - 1, edge_first, 1.0)
        self.last = jnp.where(lanes == last_lane % LANES, edge_last, 1.0)
        self.last_part = last_lane // LANES

    def depth(self, low, high):
        return quotient(high - low)

    def plane(self, value, flux_below, flux_above):
        width = value.shape[1]
        change = jnp.where(self.inner_rows, pltpu.roll(value, 7, 0) - value, 0.0)
        flux_y = quotient(change)
        change = cells(pltpu.roll(value, width - 1, 1) - value)
        change[0] = change[0] * self.first
        change[self.last_part] = change[self.last_part] * self.last
        flux_x = quotient(joined(change))
        gain = (flux_y - pltpu.roll(flux_y, 1, 0)) + (flux_x - pltpu.roll(flux_x, 1, 1))
        return value + (plane_rate * gain + depth_rate * (flux_above - flux_below))


class Place:
    def __init__(self):
        self.tm = lax.axis_index("tm")
        self.space = lax.axis_index("space")
        self.pairs = lax.axis_size("space") // 2
        self.far = (self.tm // 2) % 2
        self.slab = self.space % 2
        self.chunk = 2 * self.far + self.slab
        self.pair = self.space // 2
        self.odd = self.pair % 2

    def lower(self, slot, bit):
        value = (self.tm // (1 << bit)) % 2
        if bit == 1 and slot == 1:
            value = 1 - value
        return value == 0

    def signs(self, slot, bit, level):
        is_lower = self.lower(slot, bit)
        sign = jnp.where(is_lower, 1.0, -1.0).astype(jnp.float32)
        return sign, jnp.where(is_lower, 0.0, 0.5 * level).astype(jnp.float32)

    def sweep(self, width):
        first = jnp.where(self.chunk == 0, 0.0, 1.0).astype(jnp.float32)
        last = jnp.where(self.chunk == 3, 0.0, 1.0).astype(jnp.float32)
        return Sweep(width, first, last, width - SPARE - 1)

    def spot(self, side, distance, planes):
        is_top = self.odd == side
        return jnp.where(is_top, planes - 1 - distance, distance)

    def open_face(self, side):
        if side == 0:
            return jnp.float32(1.0)
        closed = (self.pair == 0) | (self.pair == self.pairs - 1)
        return jnp.where(closed, 0.0, 1.0).astype(jnp.float32)


def call(body, outs, *args, spaces=None, scratch=(), flops=0, smem_outs=(), grid=(), blocks=None, out_block=None):
    spaces = spaces or {}
    blocks = blocks or {}
    in_specs = [blocks.get(i, pl.BlockSpec(memory_space=spaces.get(i, VMEM))) for i in range(len(args))]
    out_specs = [out_block or pl.BlockSpec(memory_space=SMEM if i in smem_outs else VMEM) for i in range(len(outs))]
    moved = sum(a.size * 4 for a in args) + sum(o.size * 4 for o in outs)
    return pl.pallas_call(
        body,
        grid=grid,
        out_shape=outs,
        in_specs=in_specs,
        out_specs=out_specs,
        scratch_shapes=list(scratch),
        compiler_params=pltpu.CompilerParams(vmem_limit_bytes=40 << 20),
        cost_estimate=pl.CostEstimate(flops=int(flops), bytes_accessed=int(moved), transcendentals=0),
    )(*args)


def f32(*shape):
    return jax.ShapeDtypeStruct(shape, jnp.float32)


def first_kernel(own_ref, partner_ref, coeff_ref, offset_ref, level_ref, *refs):
    out_refs, whole = refs[:4], refs[4]
    planes, _, width = own_ref.shape
    place = Place()
    sign, level = place.signs(0, 0, level_ref[0])
    offset = offset_ref[0, 0, 0]
    step = width // 4
    zero = jnp.zeros((8, LANES), jnp.float32)

    def body(z, carry):
        rows = [coeff_ref[0, 0, k, pl.ds(z, 1), :] for k in range(BAND)]
        warped = warped_plane(partner_ref[z], rows, offset)
        value = haar(own_ref[z], warped, sign, level, 0.5 * root_half)
        whole[z] = joined(moved_right(cells(value) + [zero], SPARE, zero))
        return carry

    lax.fori_loop(0, planes, body, 0, unroll=2)
    for number, out_ref in enumerate(out_refs):
        start = pl.multiple_of((place.chunk ^ number) * step, LANES)
        out_ref[...] = whole[:, :, pl.ds(start, step + LANES)]


def coeff_kernel(first, coeff_ref, offset_ref, *refs):
    out_refs, whole = refs[:4], refs[4]
    planes, width = coeff_ref.shape[3:]
    place = Place()
    step = width // 4
    zero = jnp.zeros((8, LANES), jnp.float32)
    lanes = lane_ids()
    for k in range(BAND):
        for z in range(0, planes, 8):
            value = coeff_ref[0, 0, k, z : z + 8, :]
            whole[k, z : z + 8] = joined(moved_right(cells(value) + [zero], SPARE, zero))
    offset = offset_ref[0, 0, first + pl.program_id(0)].astype(jnp.float32)
    for number, out_ref in enumerate(out_refs):
        start = pl.multiple_of((place.chunk ^ number) * step, LANES)
        out_ref[0] = whole[:, :, pl.ds(start, step + LANES)]
        out_ref[0, 0, 0:8, 0:LANES] = jnp.where(lanes == 0, offset, out_ref[0, 0, 0:8, 0:LANES])


def gather_coeff_kernel(self_ref, near_ref, far_ref, across_ref, out_ref, offset_ref):
    place = Place()
    sections = self_ref.shape[0]
    for number, ref in enumerate((self_ref, near_ref, far_ref, across_ref)):
        slot = number // 2
        slab = place.slab ^ (number % 2)
        for section in range(sections):
            out_ref[section, slot, slab] = ref[section]
            corner = ref[section, 0, 0:8, 0:LANES]
            offset = jnp.max(jnp.where(lane_ids() == 0, corner, -100.0))
            offset_ref[section, slot, slab] = offset.astype(jnp.int32)


def start_kernel(self_ref, near_ref, far_ref, across_ref, state_ref, side0_ref, side1_ref):
    place = Place()
    half = self_ref.shape[0]
    planes = 2 * half
    for number, ref in enumerate((self_ref, near_ref, far_ref, across_ref)):
        slot = number // 2
        slab = place.slab ^ (number % 2)
        state_ref[slot, pl.ds(slab * half, half)] = ref[...]
    for slot in range(2):
        for side, out_ref in enumerate((side0_ref, side1_ref)):
            for e in range(EDGE):
                out_ref[slot, e] = state_ref[slot, place.spot(side, e, planes)]


def trapezoid(place, load, planes, out_ref, saved_ref, one, two):
    width = one.shape[-1]
    sweep = place.sweep(width)
    for level in range(1, SWEEPS + 1):
        def source(slot, p, level=level):
            if level == 1:
                return load(slot, p)
            return (one, two)[level % 2][slot, p]

        def put(slot, p, value, level=level):
            if level == SWEEPS:
                out_ref[slot, p - EDGE] = value
            else:
                (two, one)[level % 2][slot, p] = value

        carry = []
        for slot in range(2):
            low, here = source(slot, level - 1), source(slot, level)
            carry += [here, sweep.depth(low, here)]

        def body(i, carry):
            return step(i, carry, GROUP)

        def step(i, carry, group):
            new = []
            for slot in range(2):
                here, below = carry[2 * slot : 2 * slot + 2]
                for j in range(group):
                    p = level + GROUP * i + j
                    high = source(slot, p + 1)
                    above = sweep.depth(here, high)
                    put(slot, p, sweep.plane(here, below, above))
                    here, below = high, above
                new += [here, below]
            return new

        count = planes - 2 * level
        carry = lax.fori_loop(0, count // GROUP, body, carry)
        if count % GROUP:
            step(count // GROUP, carry, count % GROUP)
        if level < SWEEPS:
            kept = (two, one)[level % 2]
            for slot in range(2):
                for side in range(2):
                    for j in range(2):
                        spot = place.spot(side, level + j, planes)
                        saved_ref[side, slot, level - 1, j] = kept[slot, spot]


def inner_first_kernel(state_ref, out_ref, saved_ref, one, two):
    place = Place()
    trapezoid(place, lambda slot, p: state_ref[slot, p], state_ref.shape[1], out_ref, saved_ref, one, two)


def inner_kernel(section, bit, own_ref, partner_ref, side0_ref, side1_ref, coeff_ref, offset_ref, level_ref,
                 out_ref, saved_ref, zero_level, one, two):
    place = Place()
    inner = own_ref.shape[1]
    planes = inner + 2 * EDGE
    half = planes // 2
    group = 0 if section == 1 else section - 2
    for slot in range(2):
        for side, ref in enumerate((side0_ref, side1_ref)):
            for e in range(EDGE):
                zero_level[slot, place.spot(side, e, planes)] = ref[slot, e]
    for slot in range(2):
        sign, level = place.signs(slot, bit, level_ref[section])
        other = 1 - slot if bit == 1 else slot
        for slab in range(2):
            offset = offset_ref[group, slot, slab]
            start, stop = (EDGE, half) if slab == 0 else (half, planes - EDGE)

            def body(p, carry):
                rows = [coeff_ref[group, slot, slab, k, pl.ds(p - slab * half, 1), :] for k in range(BAND)]
                warped = warped_plane(partner_ref[other, p - EDGE], rows, offset)
                zero_level[slot, p] = haar(own_ref[slot, p - EDGE], warped, sign, level, root_half)
                return carry

            lax.fori_loop(start, stop, body, 0, unroll=4)
    trapezoid(place, lambda slot, p: zero_level[slot, p], planes, out_ref, saved_ref, one, two)


def wedge(place, sweep, side, slot, edge_ref, halo_ref, saved_ref):
    open_face = place.open_face(side)
    values = [halo_ref[slot, h] for h in (3, 2, 1, 0)] + [edge_ref[slot, 0], edge_ref[slot, 1]]
    for level in range(1, SWEEPS + 1):
        fluxes = [sweep.depth(a, b) for a, b in zip(values[:-1], values[1:])]
        fluxes[EDGE - level] = fluxes[EDGE - level] * open_face
        values = [sweep.plane(values[i], fluxes[i - 1], fluxes[i]) for i in range(1, 5)]
        if level < SWEEPS:
            values += [saved_ref[side, slot, level - 1, j] for j in range(2)]
    return values


def haar_edges(place, section, bit, own_ref, partner_ref, coeff_ref, offset_ref, level_ref, outs):
    half = coeff_ref.shape[4]
    group = 0 if section == 1 else section - 2
    planes = 2 * half
    for slot in range(2):
        sign, level = place.signs(slot, bit, level_ref[section])
        other = 1 - slot if bit == 1 else slot
        for side in range(2):
            slab = jnp.where(place.odd == side, 1, 0)
            offset = offset_ref[group, slot, slab]

            def body(e, carry):
                z = place.spot(side, e, planes) - slab * half
                rows = [coeff_ref[group, slot, slab, k, pl.ds(z, 1), :] for k in range(BAND)]
                warped = warped_plane(partner_ref[side, other, e], rows, offset)
                outs[side][slot, e] = haar(own_ref[side, slot, e], warped, sign, level, root_half)
                return carry

            lax.fori_loop(0, EDGE, body, 0, unroll=True)


def wedge_kernel(side0_ref, side1_ref, halo0_ref, halo1_ref, saved_ref, out_ref):
    place = Place()
    sweep = place.sweep(side0_ref.shape[-1])
    for slot in range(2):
        for side, (edge, halo) in enumerate(((side0_ref, halo0_ref), (side1_ref, halo1_ref))):
            for e, value in enumerate(wedge(place, sweep, side, slot, edge, halo, saved_ref)):
                out_ref[side, slot, e] = value


def wedge_haar_kernel(section, side0_ref, side1_ref, halo0_ref, halo1_ref, saved_ref, coeff_ref, offset_ref, level_ref,
                      out0_ref, out1_ref, kept):
    wedge_kernel(side0_ref, side1_ref, halo0_ref, halo1_ref, saved_ref, kept)
    haar_edges(Place(), section, 1, kept, kept, coeff_ref, offset_ref, level_ref, (out0_ref, out1_ref))


def haar_kernel(section, bit, own_ref, partner_ref, coeff_ref, offset_ref, level_ref, out0_ref, out1_ref):
    haar_edges(Place(), section, bit, own_ref, partner_ref, coeff_ref, offset_ref, level_ref, (out0_ref, out1_ref))


def pieces_kernel(inner_ref, edge_ref, *refs):
    out_refs, whole = refs[:4], refs[4]
    place = Place()
    inner = inner_ref.shape[1]
    planes = inner + 2 * EDGE
    half = planes // 2
    step = whole.shape[-1]
    zero = jnp.zeros((8, LANES), jnp.float32)

    def put(slot, p, value):
        whole[slot, p] = 2.0 * joined(moved_left(cells(value), SPARE)[: step // LANES])

    for slot in range(2):
        def body(p, carry):
            put(slot, p, inner_ref[slot, p - EDGE])
            return carry

        lax.fori_loop(EDGE, planes - EDGE, body, 0, unroll=4)
        for side in range(2):
            for e in range(EDGE):
                put(slot, place.spot(side, e, planes), edge_ref[side, slot, e])
    for number, out_ref in enumerate(out_refs):
        slab = place.slab ^ (number % 2)
        out_ref[...] = whole[number // 2, pl.ds(slab * half, half)]


def output_kernel(self_ref, near_ref, far_ref, across_ref, out_ref):
    place = Place()
    step = self_ref.shape[-1]
    for number, ref in enumerate((self_ref, near_ref, far_ref, across_ref)):
        start = pl.multiple_of((place.chunk ^ number) * step, LANES)
        out_ref[:, :, pl.ds(start, step)] = ref[...]


def on_device(volume, warp_coef, offsets, thresholds):
    frames, slabs = lax.axis_size("tm"), lax.axis_size("space")
    levels = frames.bit_length() - 1
    pairs = slabs // 2
    _, half, rows, length = volume.shape
    planes = 2 * half
    inner = planes - 2 * EDGE
    width = length // 4 + 2 * SPARE
    axes = ("tm", "space")

    def route(frame_bits, slab_bits):
        return [(f * slabs + s, (f ^ frame_bits) * slabs + (s ^ slab_bits)) for f in range(frames) for s in range(slabs)]

    def swap(value, frame_bits, slab_bits=0):
        return lax.ppermute(value, axes, route(frame_bits, slab_bits))

    def spread(pieces):
        return (pieces[0], swap(pieces[1], 0, 1), swap(pieces[2], 2, 0), swap(pieces[3], 2, 1))

    def halo(side0, side1):
        first = [(s, s ^ 2) for s in range(slabs)]
        second = []
        for s in range(slabs):
            pair = s // 2 + 1 if (s // 2) % 2 else s // 2 - 1
            if 0 <= pair < pairs:
                second.append((s, 2 * pair + s % 2))
        return lax.ppermute(side0, "space", first), lax.ppermute(side1, "space", second)

    state_shape = f32(2, planes, rows, width)
    side_shape = f32(2, EDGE, rows, width)
    inner_shape = f32(2, inner, rows, width)
    saved_shape = f32(2, 2, SWEEPS - 1, 2, rows, width)
    level_scratch = pltpu.VMEM((2, planes, rows, width), jnp.float32)
    sweep_flops = 8 * 2 * planes * rows * width * 30

    own_volume = volume[0]
    received = swap(own_volume, 1)

    def coeff_pieces(first, count):
        return call(
            functools.partial(coeff_kernel, first), [f32(count, BAND, half, width)] * 4, warp_coef, offsets, spaces={1: SMEM}, flops=1 << 20,
            grid=(count,),
            blocks={0: pl.BlockSpec((1, 1, BAND, half, length), lambda i: (0, first + i, 0, 0, 0))},
            out_block=pl.BlockSpec((1, BAND, half, width), lambda i: (i, 0, 0, 0)),
            scratch=[pltpu.VMEM((BAND, half, length + LANES), jnp.float32)],
        )

    def coeff_state(pieces, count):
        return call(
            gather_coeff_kernel,
            [f32(count, 2, 2, BAND, half, width), jax.ShapeDtypeStruct((count, 2, 2), jnp.int32)],
            *spread(pieces), smem_outs=(1,), flops=1 << 20,
        )

    early_coeff = coeff_pieces(1, 1)
    late_coeff = coeff_pieces(2, SECTIONS - 2)
    part = pl.BlockSpec((8, rows, length), lambda i: (i, 0, 0))
    pieces = call(
        first_kernel, [f32(half, rows, width)] * 4, own_volume, received, warp_coef, offsets, thresholds,
        spaces={3: SMEM, 4: SMEM}, flops=1 << 23, grid=(half // 8,),
        blocks={0: part, 1: part, 2: pl.BlockSpec((1, 1, BAND, 8, length), lambda i: (0, 0, 0, i, 0))},
        out_block=pl.BlockSpec((8, rows, width), lambda i: (i, 0, 0)),
        scratch=[pltpu.VMEM((8, rows, length + LANES), jnp.float32)],
    )
    state, side0, side1 = call(start_kernel, [state_shape, side_shape, side_shape], *spread(pieces), flops=1 << 20)
    halo0, halo1 = halo(side0, side1)
    early_coeff, state = lax.optimization_barrier((early_coeff, state))
    coeff, shift = coeff_state(early_coeff, 1)
    own, saved = call(
        inner_first_kernel, [inner_shape, saved_shape], state, scratch=[level_scratch] * 2, flops=sweep_flops
    )
    late_coeff, own = lax.optimization_barrier((late_coeff, own))
    later = coeff_state(late_coeff, SECTIONS - 2)
    for section in range(1, SECTIONS):
        bit = section % levels
        if section == 2:
            coeff, shift = later
        if bit == 1:
            partner = own
            side0, side1 = call(
                functools.partial(wedge_haar_kernel, section), [side_shape, side_shape],
                side0, side1, halo0, halo1, saved, coeff, shift, thresholds,
                spaces={6: SMEM, 7: SMEM}, scratch=[pltpu.VMEM((2, 2, EDGE, rows, width), jnp.float32)], flops=1 << 23,
            )
        else:
            partner = swap(own, 1 << bit)
            (edges,) = call(
                wedge_kernel, [f32(2, 2, EDGE, rows, width)], side0, side1, halo0, halo1, saved, flops=1 << 23
            )
            side0, side1 = call(
                functools.partial(haar_kernel, section, bit), [side_shape, side_shape],
                edges, swap(edges, 1 << bit), coeff, shift, thresholds, spaces={3: SMEM, 4: SMEM}, flops=1 << 22,
            )
        halo0, halo1 = halo(side0, side1)
        own, saved = call(
            functools.partial(inner_kernel, section, bit), [inner_shape, saved_shape],
            own, partner, side0, side1, coeff, shift, thresholds,
            spaces={5: SMEM, 6: SMEM}, scratch=[level_scratch] * 3, flops=sweep_flops,
        )
    (edges,) = call(
        wedge_kernel, [f32(2, 2, EDGE, rows, width)], side0, side1, halo0, halo1, saved, flops=1 << 23
    )
    pieces = call(
        pieces_kernel, [f32(half, rows, length // 4)] * 4, own, edges, flops=1 << 20,
        scratch=[pltpu.VMEM((2, planes, rows, length // 4), jnp.float32)],
    )
    (out,) = call(output_kernel, [f32(half, rows, length)], *spread(pieces), flops=1 << 20)
    return out[None]


def solution(mesh):
    return jax.shard_map(
        on_device,
        mesh=mesh,
        in_specs=(
            P("tm", "space", None, None),
            P("tm", None, None, "space", None),
            P("tm", "space", None),
            P(),
        ),
        out_specs=P("tm", "space", None, None),
        check_vma=False,
    )
```

```python
import functools

import jax
import jax.numpy as jnp
from jax import lax
from jax.experimental import pallas as pl
from jax.experimental.pallas import tpu as pltpu
from jax.sharding import PartitionSpec as P

BAND = 4
SECTIONS = 4
SWEEPS = 4
REACH = 6

depth_rate = 0.4
plane_rate = 0.05
root_half = 0.7071067811865476

LANES = 128
SPARE = 64
EDGE = SWEEPS
GROUP = 12
VMEM = pltpu.VMEM
SMEM = pltpu.SMEM


def cells(value):
    return [value[:, i : i + LANES] for i in range(0, value.shape[1], LANES)]


def joined(parts):
    return jnp.concatenate(parts, axis=1)


def lane_ids():
    return lax.broadcasted_iota(jnp.int32, (8, LANES), 1)


def quotient(change):
    return change / (1.0 + change * change)


def moved_right(parts, amount, first):
    turned = [pltpu.roll(part, amount, 1) for part in parts]
    own = lane_ids() >= amount
    ahead = [first] + turned[:-1]
    return [jnp.where(own, a, b) for a, b in zip(turned, ahead)]


def moved_left(parts, amount):
    turned = [pltpu.roll(part, (LANES - amount) % LANES, 1) for part in parts]
    own = lane_ids() < LANES - amount
    return [jnp.where(own, a, b) for a, b in zip(turned, turned[1:])]


def warped_plane(field, coeff_rows, offset):
    width = field.shape[1]
    total = None
    for band_index in range(BAND):
        shifted = pltpu.roll(field, (width + BAND // 2 - band_index - offset) % width, 1)
        term = jnp.broadcast_to(coeff_rows[band_index], shifted.shape) * shifted
        total = term if total is None else total + term
    return total


def haar(own, warped, sign, level, scale):
    value = (own + sign * warped) * scale
    return value - jnp.clip(value, -level, level)


class Sweep:
    def __init__(self, width, edge_first, edge_last, last_lane):
        rows = lax.broadcasted_iota(jnp.int32, (8, width), 0)
        self.inner_rows = rows < 7
        lanes = lane_ids()
        self.first = jnp.where(lanes == SPARE - 1, edge_first, 1.0)
        self.last = jnp.where(lanes == last_lane % LANES, edge_last, 1.0)
        self.last_part = last_lane // LANES

    def depth(self, low, high):
        return quotient(high - low)

    def plane(self, value, flux_below, flux_above):
        width = value.shape[1]
        change = jnp.where(self.inner_rows, pltpu.roll(value, 7, 0) - value, 0.0)
        flux_y = quotient(change)
        change = cells(pltpu.roll(value, width - 1, 1) - value)
        change[0] = change[0] * self.first
        change[self.last_part] = change[self.last_part] * self.last
        flux_x = quotient(joined(change))
        gain = (flux_y - pltpu.roll(flux_y, 1, 0)) + (flux_x - pltpu.roll(flux_x, 1, 1))
        return value + (plane_rate * gain + depth_rate * (flux_above - flux_below))


class Place:
    def __init__(self):
        self.tm = lax.axis_index("tm")
        self.space = lax.axis_index("space")
        self.pairs = lax.axis_size("space") // 2
        self.far = (self.tm // 2) % 2
        self.slab = self.space % 2
        self.chunk = 2 * self.far + self.slab
        self.pair = self.space // 2
        self.odd = self.pair % 2

    def lower(self, slot, bit):
        value = (self.tm // (1 << bit)) % 2
        if bit == 1 and slot == 1:
            value = 1 - value
        return value == 0

    def signs(self, slot, bit, level):
        is_lower = self.lower(slot, bit)
        sign = jnp.where(is_lower, 1.0, -1.0).astype(jnp.float32)
        return sign, jnp.where(is_lower, 0.0, 0.5 * level).astype(jnp.float32)

    def sweep(self, width):
        first = jnp.where(self.chunk == 0, 0.0, 1.0).astype(jnp.float32)
        last = jnp.where(self.chunk == 3, 0.0, 1.0).astype(jnp.float32)
        return Sweep(width, first, last, width - SPARE - 1)

    def spot(self, side, distance, planes):
        is_top = self.odd == side
        return jnp.where(is_top, planes - 1 - distance, distance)

    def open_face(self, side):
        if side == 0:
            return jnp.float32(1.0)
        closed = (self.pair == 0) | (self.pair == self.pairs - 1)
        return jnp.where(closed, 0.0, 1.0).astype(jnp.float32)


def call(body, outs, *args, spaces=None, scratch=(), micros=1.0, smem_outs=(), aliases=None, room=40):
    spaces = spaces or {}
    in_specs = [pl.BlockSpec(memory_space=spaces.get(i, VMEM)) for i in range(len(args))]
    out_specs = [pl.BlockSpec(memory_space=SMEM if i in smem_outs else VMEM) for i in range(len(outs))]
    moved = sum(a.size * 4 for a in args) + sum(o.size * 4 for o in outs)
    return pl.pallas_call(
        body,
        out_shape=outs,
        in_specs=in_specs,
        out_specs=out_specs,
        scratch_shapes=list(scratch),
        input_output_aliases=aliases or {},
        compiler_params=pltpu.CompilerParams(vmem_limit_bytes=room << 20),
        cost_estimate=pl.CostEstimate(flops=int(micros * 1.1e9), bytes_accessed=int(moved), transcendentals=0),
    )(*args)


def f32(*shape):
    return jax.ShapeDtypeStruct(shape, jnp.float32)


def fetch(copies, sems):
    started = [pltpu.make_async_copy(a, b, sems.at[i]) for i, (a, b) in enumerate(copies)]
    for copy in started:
        copy.start()
    return started


def pack_section(place, coeff_ref, offset, whole, outs):
    planes, width = coeff_ref.shape[1:]
    step = width // 4
    zero = jnp.zeros((8, LANES), jnp.float32)
    lanes = lane_ids()
    for k in range(BAND):
        for z in range(0, planes, 8):
            value = coeff_ref[k, z : z + 8, :]
            whole[k, z : z + 8] = joined(moved_right(cells(value) + [zero], SPARE, zero))
    for number, out_ref in enumerate(outs):
        start = pl.multiple_of((place.chunk ^ number) * step, LANES)
        out_ref[...] = whole[:, :, pl.ds(start, step + LANES)]
        out_ref[0, 0:8, 0:LANES] = jnp.where(lanes == 0, offset.astype(jnp.float32), out_ref[0, 0:8, 0:LANES])


def intake_kernel(coeff_hbm, offset_ref, coeff_ref, *refs):
    out_refs, (later, whole, sems) = refs[:4], refs[4:]
    now_copy, later_copy = fetch([(coeff_hbm.at[0, 0], coeff_ref), (coeff_hbm.at[0, 1], later)], sems)
    later_copy.wait()
    pack_section(Place(), later, offset_ref[0, 0, 1], whole, [ref.at[0] for ref in out_refs])
    now_copy.wait()


def coeff_kernel(first, count, coeff_hbm, offset_ref, *refs):
    out_refs, (sections, whole, sems) = refs[:4], refs[4:]
    copies = fetch([(coeff_hbm.at[0, first + i], sections.at[i]) for i in range(count)], sems)
    for i in range(count):
        copies[i].wait()
        pack_section(Place(), sections.at[i], offset_ref[0, 0, first + i], whole, [ref.at[i] for ref in out_refs])


def first_kernel(own_ref, partner_ref, coeff_ref, offset_ref, level_ref, *refs):
    out_refs, whole = refs[:4], refs[4]
    planes, _, width = own_ref.shape
    place = Place()
    sign, level = place.signs(0, 0, level_ref[0])
    offset = offset_ref[0, 0, 0]
    step = width // 4
    zero = jnp.zeros((8, LANES), jnp.float32)
    no_rows = jnp.zeros((1, LANES), jnp.float32)

    def body(z, carry):
        field = joined([partner_ref[z], zero])
        width = field.shape[1]
        shifted = pltpu.roll(field, (width + BAND // 2 - offset) % width, 1)
        warped = None
        for k in range(BAND):
            row = joined([coeff_ref[k, pl.ds(z, 1), :], no_rows])
            term = jnp.broadcast_to(row, shifted.shape) * (pltpu.roll(shifted, width - k, 1) if k else shifted)
            warped = term if warped is None else warped + term
        value = haar(joined([own_ref[z], zero]), warped, sign, level, 0.5 * root_half)
        whole[z] = pltpu.roll(value, SPARE, 1)
        return carry

    lax.fori_loop(0, planes, body, 0, unroll=2)
    for number, out_ref in enumerate(out_refs):
        start = pl.multiple_of((place.chunk ^ number) * step, LANES)
        out_ref[...] = whole[:, :, pl.ds(start, step + LANES)]


def gather_coeff_kernel(self_ref, near_ref, far_ref, across_ref, out_ref, offset_ref):
    place = Place()
    sections = self_ref.shape[0]
    for number, ref in enumerate((self_ref, near_ref, far_ref, across_ref)):
        slot = number // 2
        slab = place.slab ^ (number % 2)
        for section in range(sections):
            out_ref[section, slot, slab] = ref[section]
            corner = ref[section, 0, 0:8, 0:LANES]
            offset = jnp.max(jnp.where(lane_ids() == 0, corner, -100.0))
            offset_ref[section, slot, slab] = offset.astype(jnp.int32)


def start_kernel(self_ref, near_ref, far_ref, across_ref, side0_ref, side1_ref):
    place = Place()
    half = self_ref.shape[0]
    for side, out_ref in enumerate((side0_ref, side1_ref)):
        is_top = place.odd == side
        slab = jnp.where(is_top, 1, 0)
        for own_slab in (True, False):
            pieces = (self_ref, far_ref) if own_slab else (near_ref, across_ref)

            @pl.when((slab == place.slab) == own_slab)
            def _():
                for slot, piece in enumerate(pieces):
                    for e in range(EDGE):
                        out_ref[slot, e] = piece[jnp.where(is_top, half - 1 - e, e)]


def trapezoid(place, load, planes, emit, saved_ref, one, two, slots=(0, 1)):
    width = one.shape[-1]
    sweep = place.sweep(width)
    size = GROUP // len(slots)
    for level in range(1, SWEEPS + 1):
        def source(slot, p, level=level):
            if level == 1:
                return load(slot, p)
            return (one, two)[level % 2][slot, p]

        def put(slot, p, value, level=level):
            if level == SWEEPS:
                emit(slot, p - EDGE, value)
            else:
                (two, one)[level % 2][slot, p] = value

        carry = []
        for slot in slots:
            low, here = source(slot, level - 1), source(slot, level)
            carry += [here, sweep.depth(low, here)]

        def body(i, carry):
            return step(i, carry, size)

        def step(i, carry, group):
            new = []
            for slot in slots:
                at = 2 * slots.index(slot)
                here, below = carry[at : at + 2]
                for j in range(group):
                    p = level + size * i + j
                    high = source(slot, p + 1)
                    above = sweep.depth(here, high)
                    put(slot, p, sweep.plane(here, below, above))
                    here, below = high, above
                new += [here, below]
            return new

        count = planes - 2 * level
        carry = lax.fori_loop(0, count // size, body, carry)
        if count % size:
            step(count // size, carry, count % size)
        if level < SWEEPS:
            kept = (two, one)[level % 2]
            for slot in slots:
                for side in range(2):
                    for j in range(2):
                        spot = place.spot(side, level + j, planes)
                        saved_ref[side, slot % saved_ref.shape[1], level - 1, j] = kept[slot, spot]


def inner_first_kernel(slot, own_ref, other_ref, *refs):
    out_ref, saved_ref, state, one, two = refs[-5:]
    place = Place()
    half = own_ref.shape[0]
    state[slot, pl.ds(place.slab * half, half)] = own_ref[...]
    state[slot, pl.ds((1 - place.slab) * half, half)] = other_ref[...]

    def emit(slot, i, value):
        out_ref[slot, i] = value

    trapezoid(place, lambda slot, p: state[slot, p], 2 * half, emit, saved_ref, one, two, (slot,))


def finished(value):
    return 2.0 * joined(moved_left(cells(value), SPARE)[: (value.shape[1] - 2 * SPARE) // LANES])


def inner_haar(place, section, bit, slots, own_ref, partner_ref, sides, coeff_ref, offset_ref, level_ref, zero_level):
    inner = own_ref.shape[1]
    planes = inner + 2 * EDGE
    half = planes // 2
    group = 0 if section == 1 else section - 2
    for slot in slots:
        for side, ref in enumerate(sides):
            for e in range(EDGE):
                zero_level[slot, place.spot(side, e, planes)] = ref[slot, e]
    for slot in slots:
        sign, level = place.signs(slot, bit, level_ref[section])
        other = 1 - slot if bit == 1 else slot
        for slab in range(2):
            offset = offset_ref[group, slot, slab]
            start, stop = (EDGE, half) if slab == 0 else (half, planes - EDGE)
            for p in range(start, stop):
                rows = [coeff_ref[group, slot, slab, k, pl.ds(p - slab * half, 1), :] for k in range(BAND)]
                warped = warped_plane(partner_ref[other, p - EDGE], rows, offset)
                zero_level[slot, p] = haar(own_ref[slot, p - EDGE], warped, sign, level, root_half)


def inner_kernel(section, bit, own_ref, partner_ref, side0_ref, side1_ref, coeff_ref, offset_ref, level_ref,
                 out_ref, saved_ref, zero_level, one, two):
    place = Place()
    planes = own_ref.shape[1] + 2 * EDGE
    sides = (side0_ref, side1_ref)
    inner_haar(place, section, bit, (0, 1), own_ref, partner_ref, sides, coeff_ref, offset_ref, level_ref, zero_level)

    def emit(slot, i, value):
        out_ref[slot, i] = value

    trapezoid(place, lambda slot, p: zero_level[slot, p], planes, emit, saved_ref, one, two)


def inner_last_kernel(section, bit, slot, own_ref, partner_ref, side0_ref, side1_ref, coeff_ref, offset_ref, level_ref,
                      mine_ref, other_ref, saved_ref, zero_level, one, two, done):
    place = Place()
    planes = own_ref.shape[1] + 2 * EDGE
    sides = (side0_ref, side1_ref)
    inner_haar(place, section, bit, (slot,), own_ref, partner_ref, sides, coeff_ref, offset_ref, level_ref, zero_level)

    def emit(slot, i, value):
        done[i] = finished(value)

    trapezoid(place, lambda slot, p: zero_level[slot, p], planes, emit, saved_ref, one, two, (slot,))
    count = mine_ref.shape[0]
    mine_ref[...] = done[pl.ds(place.slab * count, count)]
    other_ref[...] = done[pl.ds((1 - place.slab) * count, count)]


def wedge(place, sweep, side, edge_ref, halo_ref, saved):
    open_face = place.open_face(side)
    values = [
        [halo_ref[slot, h] for h in (3, 2, 1, 0)] + [edge_ref[slot, 0], edge_ref[slot, 1]] for slot in range(2)
    ]
    for level in range(1, SWEEPS + 1):
        for slot in range(2):
            here = values[slot]
            fluxes = [sweep.depth(a, b) for a, b in zip(here[:-1], here[1:])]
            fluxes[EDGE - level] = fluxes[EDGE - level] * open_face
            here = [sweep.plane(here[i], fluxes[i - 1], fluxes[i]) for i in range(1, 5)]
            if level < SWEEPS:
                here += [saved(side, slot, level - 1, j) for j in range(2)]
            values[slot] = here
    return values


def wedge_kernel(side0_ref, side1_ref, halo0_ref, halo1_ref, saved_ref, out_ref):
    place = Place()
    sweep = place.sweep(side0_ref.shape[-1])
    for side, (edge, halo) in enumerate(((side0_ref, halo0_ref), (side1_ref, halo1_ref))):
        values = wedge(place, sweep, side, edge, halo, lambda *at: saved_ref[at])
        for slot in range(2):
            for e in range(EDGE):
                out_ref[side, slot, e] = values[slot][e]


def haar_kernel(section, bit, own_ref, partner_ref, coeff_ref, offset_ref, level_ref, out0_ref, out1_ref):
    place = Place()
    outs = (out0_ref, out1_ref)
    half = coeff_ref.shape[4]
    group = 0 if section == 1 else section - 2
    planes = 2 * half
    for slot in range(2):
        sign, level = place.signs(slot, bit, level_ref[section])
        other = 1 - slot if bit == 1 else slot
        for side in range(2):
            slab = jnp.where(place.odd == side, 1, 0)
            offset = offset_ref[group, slot, slab]
            for e in range(EDGE):
                z = place.spot(side, e, planes) - slab * half
                rows = [coeff_ref[group, slot, slab, k, pl.ds(z, 1), :] for k in range(BAND)]
                warped = warped_plane(partner_ref[side, other, e], rows, offset)
                outs[side][slot, e] = haar(own_ref[side, slot, e], warped, sign, level, root_half)


def wedge_last_kernel(side0_ref, side1_ref, halo0_ref, halo1_ref, saved0_ref, saved1_ref, *refs):
    out_refs, done = refs[:4], refs[4]
    place = Place()
    sweep = place.sweep(side0_ref.shape[-1])
    saved_refs = (saved0_ref, saved1_ref)

    def saved(side, slot, level, j):
        return saved_refs[slot][side, 0, level, j]

    for side, (edge, halo) in enumerate(((side0_ref, halo0_ref), (side1_ref, halo1_ref))):
        values = wedge(place, sweep, side, edge, halo, saved)
        for slot in range(2):
            for e in range(EDGE):
                done[side, slot, e] = finished(values[slot][e])
    for number, out_ref in enumerate(out_refs):
        slab = place.slab ^ (number % 2)
        side = jnp.where(slab == 1, place.odd, 1 - place.odd)
        out_ref[...] = done[side, number // 2]


def output_kernel(*refs):
    inner_refs, edge_refs, out_ref = refs[:4], refs[4:8], refs[8]
    place = Place()
    half = out_ref.shape[0]
    inner, _, step = inner_refs[0].shape
    for number in range(4):
        lanes = pl.ds(pl.multiple_of((place.chunk ^ number) * step, LANES), step)
        out_ref[pl.ds((1 - place.slab) * EDGE, inner), :, lanes] = inner_refs[number][...]
        for e in range(EDGE):
            out_ref[jnp.where(place.slab == 1, half - 1 - e, e), :, lanes] = edge_refs[number][e]


def on_device(volume, warp_coef, offsets, thresholds):
    frames, slabs = lax.axis_size("tm"), lax.axis_size("space")
    levels = frames.bit_length() - 1
    pairs = slabs // 2
    _, half, rows, length = volume.shape
    planes = 2 * half
    inner = planes - 2 * EDGE
    width = length // 4 + 2 * SPARE
    axes = ("tm", "space")

    def route(frame_bits, slab_bits):
        return [(f * slabs + s, (f ^ frame_bits) * slabs + (s ^ slab_bits)) for f in range(frames) for s in range(slabs)]

    def swap(value, frame_bits, slab_bits=0):
        return lax.ppermute(value, axes, route(frame_bits, slab_bits))

    def spread(pieces):
        return (pieces[0], swap(pieces[1], 0, 1), swap(pieces[2], 2, 0), swap(pieces[3], 2, 1))

    def halo(side0, side1):
        first = [(s, s ^ 2) for s in range(slabs)]
        second = []
        for s in range(slabs):
            pair = s // 2 + 1 if (s // 2) % 2 else s // 2 - 1
            if 0 <= pair < pairs:
                second.append((s, 2 * pair + s % 2))
        return lax.ppermute(side0, "space", first), lax.ppermute(side1, "space", second)

    side_shape = f32(2, EDGE, rows, width)
    inner_shape = f32(2, inner, rows, width)
    saved_shape = f32(2, 2, SWEEPS - 1, 2, rows, width)
    edges_shape = f32(2, 2, EDGE, rows, width)
    level_scratch = pltpu.VMEM((2, planes, rows, width), jnp.float32)
    packed = pltpu.VMEM((BAND, half, length + LANES), jnp.float32)

    def coeff_state(pieces, count):
        return call(
            gather_coeff_kernel,
            [f32(count, 2, 2, BAND, half, width), jax.ShapeDtypeStruct((count, 2, 2), jnp.int32)],
            *pieces, smem_outs=(1,), micros=0.8,
        )

    received = swap(volume[0], 1)
    first_coeff, *early = call(
        intake_kernel, [f32(BAND, half, length)] + [f32(1, BAND, half, width)] * 4, warp_coef, offsets,
        spaces={0: pltpu.HBM, 1: SMEM}, micros=1.2,
        scratch=[pltpu.VMEM((BAND, half, length), jnp.float32), packed, pltpu.SemaphoreType.DMA((2,))],
    )
    early = spread(early)
    late_count = SECTIONS - 2
    pieces = call(
        first_kernel, [f32(half, rows, width)] * 4, volume[0], received, first_coeff, offsets, thresholds,
        spaces={3: SMEM, 4: SMEM}, micros=4.0, scratch=[pltpu.VMEM((half, rows, length + LANES), jnp.float32)],
    )
    pieces, early = lax.optimization_barrier((pieces, early))
    late = call(
        functools.partial(coeff_kernel, 2, late_count), [f32(late_count, BAND, half, width)] * 4, warp_coef, offsets,
        spaces={0: pltpu.HBM, 1: SMEM}, micros=1.5,
        scratch=[
            pltpu.VMEM((late_count, BAND, half, length), jnp.float32), packed, pltpu.SemaphoreType.DMA((late_count,)),
        ],
    )
    mine, near, far = pieces[0], swap(pieces[1], 0, 1), swap(pieces[2], 2, 0)
    last, near, far = lax.optimization_barrier((pieces[3], near, far))
    across = swap(last, 2, 1)
    own, saved = call(
        functools.partial(inner_first_kernel, 0), [inner_shape, saved_shape], mine, near,
        scratch=[level_scratch] * 3, micros=3.5,
    )
    across, own = lax.optimization_barrier((across, own))
    side0, side1 = call(start_kernel, [side_shape, side_shape], mine, near, far, across, micros=0.2)
    late, side0 = lax.optimization_barrier((late, side0))
    halo0, halo1 = halo(side0, side1)
    own, saved = call(
        functools.partial(inner_first_kernel, 1), [inner_shape, saved_shape], far, across, own, saved,
        scratch=[level_scratch] * 3, micros=3.5, aliases={2: 0, 3: 1},
    )
    late = spread(late)
    coeff, shift = coeff_state(early, 1)
    for section in range(1, SECTIONS):
        bit = section % levels
        (edges,) = call(wedge_kernel, [edges_shape], side0, side1, halo0, halo1, saved, micros=2.4)
        partner, partner_edges = own, edges
        if bit != 1:
            partner, edges = lax.optimization_barrier((own, edges))
            partner, partner_edges = swap(partner, 1 << bit), swap(edges, 1 << bit)
        side0, side1 = call(
            functools.partial(haar_kernel, section, bit), [side_shape, side_shape],
            edges, partner_edges, coeff, shift, thresholds, spaces={3: SMEM, 4: SMEM}, micros=1.1,
        )
        used = coeff, shift
        if section == 1:
            late, side0, side1 = lax.optimization_barrier((late, side0, side1))
            coeff, shift = coeff_state(late, late_count)
        halo0, halo1 = halo(side0, side1)
        if section == SECTIONS - 1:
            break
        own, saved = call(
            functools.partial(inner_kernel, section, bit), [inner_shape, saved_shape],
            own, partner, side0, side1, *used, thresholds,
            spaces={5: SMEM, 6: SMEM}, scratch=[level_scratch] * 3, micros=8.0,
        )
    piece_shape = f32(half - EDGE, rows, length // 4)
    edge_shape = f32(EDGE, rows, length // 4)
    slot_saved = f32(2, 1, SWEEPS - 1, 2, rows, width)

    def last_inner(slot):
        return call(
            functools.partial(inner_last_kernel, section, bit, slot), [piece_shape, piece_shape, slot_saved],
            own, partner, side0, side1, *used, thresholds, spaces={5: SMEM, 6: SMEM}, micros=4.2,
            scratch=[level_scratch] * 3 + [pltpu.VMEM((inner, rows, length // 4), jnp.float32)],
        )

    far, across, saved1 = last_inner(1)
    across = swap(across, 2, 1)
    mine, near, saved0 = last_inner(0)
    across, halo0 = lax.optimization_barrier((across, halo0))
    inners = (mine, swap(near, 0, 1), swap(far, 2, 0), across)
    edges = call(
        wedge_last_kernel, [edge_shape] * 4, side0, side1, halo0, halo1, saved0, saved1, micros=2.5,
        scratch=[pltpu.VMEM((2, 2, EDGE, rows, length // 4), jnp.float32)],
    )
    (out,) = call(output_kernel, [f32(half, rows, length)], *inners, *spread(edges), micros=1.0)
    return out[None]


def solution(mesh):
    return jax.shard_map(
        on_device,
        mesh=mesh,
        in_specs=(
            P("tm", "space", None, None),
            P("tm", None, None, "space", None),
            P("tm", "space", None),
            P(),
        ),
        out_specs=P("tm", "space", None, None),
        check_vma=False,
    )
```

```python
import functools

import jax
import jax.numpy as jnp
from jax import lax
from jax.experimental import pallas as pl
from jax.experimental.pallas import tpu as pltpu
from jax.sharding import PartitionSpec as P

BAND = 4
SECTIONS = 4
SWEEPS = 4
REACH = 6

depth_rate = 0.4
plane_rate = 0.05
root_half = 0.7071067811865476

LANES = 128
HELD = (0.25 / plane_rate) ** 0.5
SPARE = 64
EDGE = SWEEPS
GROUP = {1: 12, 2: 8}
VMEM = pltpu.VMEM
SMEM = pltpu.SMEM


def cells(value):
    return [value[:, i : i + LANES] for i in range(0, value.shape[1], LANES)]


def joined(parts):
    return jnp.concatenate(parts, axis=1)


def lane_ids():
    return lax.broadcasted_iota(jnp.int32, (8, LANES), 1)


def quotient(change):
    return change / (1.0 / plane_rate + change * change)


def moved_right(parts, amount, first):
    turned = [pltpu.roll(part, amount, 1) for part in parts]
    own = lane_ids() >= amount
    ahead = [first] + turned[:-1]
    return [jnp.where(own, a, b) for a, b in zip(turned, ahead)]


def moved_left(parts, amount):
    turned = [pltpu.roll(part, (LANES - amount) % LANES, 1) for part in parts]
    own = lane_ids() < LANES - amount
    return [jnp.where(own, a, b) for a, b in zip(turned, turned[1:])]


def warped_plane(field, coeff_rows, offset):
    width = field.shape[1]
    total = None
    for band_index in range(BAND):
        shifted = pltpu.roll(field, (width + BAND // 2 - band_index - offset) % width, 1)
        term = jnp.broadcast_to(coeff_rows[band_index], shifted.shape) * shifted
        total = term if total is None else total + term
    return total


def haar(own, warped, sign, level, scale):
    value = (own + sign * warped) * scale
    return value - jnp.clip(value, -level, level)


class Sweep:
    def __init__(self, width, edge_first, edge_last, last_lane):
        rows = lax.broadcasted_iota(jnp.int32, (8, width), 0)
        self.inner_rows = rows < 7
        lanes = lane_ids()
        self.first = jnp.where(lanes == SPARE - 1, edge_first, 1.0)
        self.last = jnp.where(lanes == last_lane % LANES, edge_last, 1.0)
        self.last_part = last_lane // LANES

    def depth(self, low, high):
        return quotient(high - low)

    def plane(self, value, flux_below, flux_above):
        width = value.shape[1]
        change = jnp.where(self.inner_rows, pltpu.roll(value, 7, 0) - value, 0.0)
        flux_y = quotient(change)
        change = cells(pltpu.roll(value, width - 1, 1) - value)
        change[0] = change[0] * self.first
        change[self.last_part] = change[self.last_part] * self.last
        flux_x = quotient(joined(change))
        gain = (flux_y - pltpu.roll(flux_y, 1, 0)) + (flux_x - pltpu.roll(flux_x, 1, 1))
        return value + (gain + (depth_rate / plane_rate) * (flux_above - flux_below))


class Place:
    def __init__(self):
        self.tm = lax.axis_index("tm")
        self.space = lax.axis_index("space")
        self.pairs = lax.axis_size("space") // 2
        self.far = (self.tm // 2) % 2
        self.slab = self.space % 2
        self.chunk = 2 * self.far + self.slab
        self.pair = self.space // 2
        self.odd = self.pair % 2

    def lower(self, slot, bit):
        value = (self.tm // (1 << bit)) % 2
        if bit == 1 and slot == 1:
            value = 1 - value
        return value == 0

    def signs(self, slot, bit, level):
        is_lower = self.lower(slot, bit)
        sign = jnp.where(is_lower, 1.0, -1.0).astype(jnp.float32)
        return sign, jnp.where(is_lower, 0.0, HELD * level).astype(jnp.float32)

    def sweep(self, width):
        first = jnp.where(self.chunk == 0, 0.0, 1.0).astype(jnp.float32)
        last = jnp.where(self.chunk == 3, 0.0, 1.0).astype(jnp.float32)
        return Sweep(width, first, last, width - SPARE - 1)

    def spot(self, side, distance, planes):
        is_top = self.odd == side
        return jnp.where(is_top, planes - 1 - distance, distance)

    def open_face(self, side):
        if side == 0:
            return jnp.float32(1.0)
        closed = (self.pair == 0) | (self.pair == self.pairs - 1)
        return jnp.where(closed, 0.0, 1.0).astype(jnp.float32)


def call(body, outs, *args, spaces=None, scratch=(), micros=1.0, smem_outs=(), aliases=None, room=40):
    spaces = spaces or {}
    in_specs = [pl.BlockSpec(memory_space=spaces.get(i, VMEM)) for i in range(len(args))]
    out_specs = [pl.BlockSpec(memory_space=SMEM if i in smem_outs else VMEM) for i in range(len(outs))]
    moved = sum(a.size * 4 for a in args) + sum(o.size * 4 for o in outs)
    return pl.pallas_call(
        body,
        out_shape=outs,
        in_specs=in_specs,
        out_specs=out_specs,
        scratch_shapes=list(scratch),
        input_output_aliases=aliases or {},
        compiler_params=pltpu.CompilerParams(vmem_limit_bytes=room << 20),
        cost_estimate=pl.CostEstimate(flops=int(micros * 1.1e9), bytes_accessed=int(moved), transcendentals=0),
    )(*args)


def f32(*shape):
    return jax.ShapeDtypeStruct(shape, jnp.float32)


def marked(value, offset):
    return jnp.where(lane_ids() == 0, offset.astype(jnp.float32), value)


def pack_section(place, coeff_ref, whole, outs):
    planes, width = coeff_ref.shape[1:]
    step = width // 4
    zero = jnp.zeros((8, LANES), jnp.float32)
    for k in range(BAND):
        for z in range(0, planes, 8):
            value = coeff_ref[k, z : z + 8, :]
            whole[k, z : z + 8] = joined(moved_right(cells(value) + [zero], SPARE, zero))
    for number, out_ref in enumerate(outs):
        start = pl.multiple_of((place.chunk ^ number) * step, LANES)
        out_ref[...] = whole[:, :, pl.ds(start, step + LANES)]


def early_kernel(coeff_ref, *refs):
    pack_section(Place(), coeff_ref, refs[4], refs[:4])


def late_kernel(coeff_ref, offset_ref, *refs):
    for section in range(2, SECTIONS):
        outs = [ref.at[section - 2] for ref in refs[:4]]
        pack_section(Place(), coeff_ref.at[0, section], refs[4], outs)
        for out in outs:
            out[0, 0:8, 0:LANES] = marked(out[0, 0:8, 0:LANES], offset_ref[0, 0, section])


def first_kernel(own_ref, partner_ref, coeff_ref, offset_ref, level_ref, *refs):
    out_refs, whole = refs[:4], refs[4]
    planes, _, width = own_ref.shape
    place = Place()
    sign, level = place.signs(0, 0, level_ref[0])
    offset = offset_ref[0, 0, 0]
    step = width // 4
    zero = jnp.zeros((8, LANES), jnp.float32)
    no_rows = jnp.zeros((1, LANES), jnp.float32)

    def body(z, carry):
        field = joined([partner_ref[z], zero])
        width = field.shape[1]
        shifted = pltpu.roll(field, (width + BAND // 2 - offset) % width, 1)
        warped = None
        for k in range(BAND):
            row = joined([coeff_ref[0, 0, k, pl.ds(z, 1), :], no_rows])
            term = jnp.broadcast_to(row, shifted.shape) * (pltpu.roll(shifted, width - k, 1) if k else shifted)
            warped = term if warped is None else warped + term
        value = haar(joined([own_ref[z], zero]), warped, sign, level, HELD * root_half)
        whole[z] = pltpu.roll(value, SPARE, 1)
        return carry

    lax.fori_loop(0, planes, body, 0, unroll=2)
    for number, out_ref in enumerate(out_refs):
        start = pl.multiple_of((place.chunk ^ number) * step, LANES)
        out_ref[...] = whole[:, :, pl.ds(start, step + LANES)]
        out_ref[0, :, 0:LANES] = marked(out_ref[0, :, 0:LANES], offset_ref[0, 0, 1])


def coeff_rows(section, refs):
    if section == 1:
        return [lambda k, z, ref=ref: ref[k, pl.ds(z, 1), :] for ref in refs]
    return [lambda k, z, ref=ref: ref[section - 2, k, pl.ds(z, 1), :] for ref in refs]


def start_kernel(self_ref, near_ref, far_ref, across_ref, side0_ref, side1_ref):
    place = Place()
    half = self_ref.shape[0]
    for side, out_ref in enumerate((side0_ref, side1_ref)):
        is_top = place.odd == side
        slab = jnp.where(is_top, 1, 0)
        for own_slab in (True, False):
            pieces = (self_ref, far_ref) if own_slab else (near_ref, across_ref)

            @pl.when((slab == place.slab) == own_slab)
            def _():
                for slot, piece in enumerate(pieces):
                    for e in range(EDGE):
                        out_ref[slot, e] = piece[jnp.where(is_top, half - 1 - e, e)]


def trapezoid(place, load, planes, emit, saved_ref, one, two, slots=(0, 1)):
    width = one.shape[-1]
    sweep = place.sweep(width)
    size = GROUP[len(slots)]
    for level in range(1, SWEEPS + 1):
        def source(slot, p, level=level):
            if level == 1:
                return load(slot, p)
            return (one, two)[level % 2][slot, p]

        def put(slot, p, value, level=level):
            if level == SWEEPS:
                emit(slot, p - EDGE, value)
            else:
                (two, one)[level % 2][slot, p] = value

        carry = []
        for slot in slots:
            low, here = source(slot, level - 1), source(slot, level)
            carry += [here, sweep.depth(low, here)]

        def body(i, carry):
            return step(i, carry, size)

        def step(i, carry, group):
            new = []
            for slot in slots:
                at = 2 * slots.index(slot)
                here, below = carry[at : at + 2]
                for j in range(group):
                    p = level + size * i + j
                    high = source(slot, p + 1)
                    above = sweep.depth(here, high)
                    put(slot, p, sweep.plane(here, below, above))
                    here, below = high, above
                new += [here, below]
            return new

        count = planes - 2 * level
        carry = lax.fori_loop(0, count // size, body, carry)
        if count % size:
            step(count // size, carry, count % size)
        if level < SWEEPS:
            kept = (two, one)[level % 2]
            for slot in slots:
                for side in range(2):
                    for j in range(2):
                        spot = place.spot(side, level + j, planes)
                        saved_ref[side, slot % saved_ref.shape[1], level - 1, j] = kept[slot, spot]


def inner_first_kernel(slot, own_ref, other_ref, *refs):
    out_ref, saved_ref, state, one, two = refs[-5:]
    place = Place()
    half = own_ref.shape[0]
    state[slot, pl.ds(place.slab * half, half)] = own_ref[...]
    state[slot, pl.ds((1 - place.slab) * half, half)] = other_ref[...]

    def emit(slot, i, value):
        out_ref[slot, i] = value

    trapezoid(place, lambda slot, p: state[slot, p], 2 * half, emit, saved_ref, one, two, (slot,))


def finished(value):
    return (1.0 / HELD) * joined(moved_left(cells(value), SPARE)[: (value.shape[1] - 2 * SPARE) // LANES])


def inner_haar(place, section, bit, slots, own_ref, partner_ref, sides, coeff_refs, offset_ref, level_ref, zero_level):
    inner = own_ref.shape[1]
    planes = inner + 2 * EDGE
    half = planes // 2
    rows_of = coeff_rows(section, coeff_refs)
    for slot in slots:
        for side, ref in enumerate(sides):
            for e in range(EDGE):
                zero_level[slot, place.spot(side, e, planes)] = ref[slot, e]
    for slot in slots:
        sign, level = place.signs(slot, bit, level_ref[section])
        other = 1 - slot if bit == 1 else slot
        for away in range(2):
            slab = place.slab ^ away
            offset = offset_ref[0 if section == 1 else section - 2, slot, away]
            start = jnp.where(slab == 0, EDGE, 0)
            for i in range(half - EDGE):
                z = start + i
                p = slab * half + z
                rows = [rows_of[2 * slot + away](k, z) for k in range(BAND)]
                warped = warped_plane(partner_ref[other, p - EDGE], rows, offset)
                zero_level[slot, p] = haar(own_ref[slot, p - EDGE], warped, sign, level, root_half)


def inner_kernel(section, bit, own_ref, partner_ref, side0_ref, side1_ref, offset_ref, level_ref, *refs):
    coeff_refs, (out_ref, saved_ref, zero_level, one, two) = refs[:4], refs[4:]
    place = Place()
    planes = own_ref.shape[1] + 2 * EDGE
    sides = (side0_ref, side1_ref)
    inner_haar(place, section, bit, (0, 1), own_ref, partner_ref, sides, coeff_refs, offset_ref, level_ref, zero_level)

    def emit(slot, i, value):
        out_ref[slot, i] = value

    trapezoid(place, lambda slot, p: zero_level[slot, p], planes, emit, saved_ref, one, two)


def inner_last_kernel(section, bit, slot, own_ref, partner_ref, side0_ref, side1_ref, offset_ref, level_ref, *refs):
    coeff_refs, (mine_ref, other_ref, saved_ref, zero_level, one, two, done) = refs[:4], refs[4:]
    place = Place()
    planes = own_ref.shape[1] + 2 * EDGE
    sides = (side0_ref, side1_ref)
    inner_haar(place, section, bit, (slot,), own_ref, partner_ref, sides, coeff_refs, offset_ref, level_ref, zero_level)

    def emit(slot, i, value):
        done[i] = finished(value)

    trapezoid(place, lambda slot, p: zero_level[slot, p], planes, emit, saved_ref, one, two, (slot,))
    count = mine_ref.shape[0]
    mine_ref[...] = done[pl.ds(place.slab * count, count)]
    other_ref[...] = done[pl.ds((1 - place.slab) * count, count)]


def wedge(place, sweep, side, edge_ref, halo_ref, saved):
    open_face = place.open_face(side)
    values = [
        [halo_ref[slot, h] for h in (3, 2, 1, 0)] + [edge_ref[slot, 0], edge_ref[slot, 1]] for slot in range(2)
    ]
    for level in range(1, SWEEPS + 1):
        for slot in range(2):
            here = values[slot]
            fluxes = [sweep.depth(a, b) for a, b in zip(here[:-1], here[1:])]
            fluxes[EDGE - level] = fluxes[EDGE - level] * open_face
            here = [sweep.plane(here[i], fluxes[i - 1], fluxes[i]) for i in range(1, 5)]
            if level < SWEEPS:
                here += [saved(side, slot, level - 1, j) for j in range(2)]
            values[slot] = here
    return values


def wedge_kernel(corners, side0_ref, side1_ref, halo0_ref, halo1_ref, saved_ref, *refs):
    marked_refs, out_ref = refs[: 4 * bool(corners)], refs[4 * bool(corners)]
    place = Place()
    sweep = place.sweep(side0_ref.shape[-1])
    for number, ref in enumerate(marked_refs):
        for i, at in enumerate(corners):
            value = jnp.max(jnp.where(lane_ids() == 0, ref[*at, 0:8, 0:LANES], -100.0))
            refs[5][i, number // 2, number % 2] = value.astype(jnp.int32)
    for side, (edge, halo) in enumerate(((side0_ref, halo0_ref), (side1_ref, halo1_ref))):
        values = wedge(place, sweep, side, edge, halo, lambda *at: saved_ref[at])
        for slot in range(2):
            for e in range(EDGE):
                out_ref[side, slot, e] = values[slot][e]


def haar_kernel(section, bit, own_ref, partner_ref, offset_ref, level_ref, *refs):
    coeff_refs, (out0_ref, out1_ref, done) = refs[:4], refs[4:]
    place = Place()
    half = coeff_refs[0].shape[-2]
    rows_of = coeff_rows(section, coeff_refs)
    for slot in range(2):
        sign, level = place.signs(slot, bit, level_ref[section])
        other = 1 - slot if bit == 1 else slot
        for away in range(2):
            is_top = place.slab ^ away == 1
            side = jnp.where(is_top, place.odd, 1 - place.odd)
            offset = offset_ref[0 if section == 1 else section - 2, slot, away]
            for e in range(EDGE):
                z = jnp.where(is_top, half - 1 - e, e)
                rows = [rows_of[2 * slot + away](k, z) for k in range(BAND)]
                warped = warped_plane(partner_ref[side, other, e], rows, offset)
                done[side, slot, e] = haar(own_ref[side, slot, e], warped, sign, level, root_half)
    out0_ref[...] = done[0]
    out1_ref[...] = done[1]


def wedge_last_kernel(side0_ref, side1_ref, halo0_ref, halo1_ref, saved0_ref, saved1_ref, *refs):
    out_refs, done = refs[:4], refs[4]
    place = Place()
    sweep = place.sweep(side0_ref.shape[-1])
    saved_refs = (saved0_ref, saved1_ref)

    def saved(side, slot, level, j):
        return saved_refs[slot][side, 0, level, j]

    for side, (edge, halo) in enumerate(((side0_ref, halo0_ref), (side1_ref, halo1_ref))):
        values = wedge(place, sweep, side, edge, halo, saved)
        for slot in range(2):
            for e in range(EDGE):
                done[side, slot, e] = finished(values[slot][e])
    for number, out_ref in enumerate(out_refs):
        slab = place.slab ^ (number % 2)
        side = jnp.where(slab == 1, place.odd, 1 - place.odd)
        out_ref[...] = done[side, number // 2]


def output_kernel(*refs):
    inner_refs, edge_refs, out_ref = refs[:4], refs[4:8], refs[8]
    place = Place()
    half = out_ref.shape[0]
    inner, _, step = inner_refs[0].shape
    for number in range(4):
        lanes = pl.ds(pl.multiple_of((place.chunk ^ number) * step, LANES), step)
        out_ref[pl.ds((1 - place.slab) * EDGE, inner), :, lanes] = inner_refs[number][...]
        for e in range(EDGE):
            out_ref[jnp.where(place.slab == 1, half - 1 - e, e), :, lanes] = edge_refs[number][e]


def on_device(volume, warp_coef, offsets, thresholds):
    frames, slabs = lax.axis_size("tm"), lax.axis_size("space")
    levels = frames.bit_length() - 1
    pairs = slabs // 2
    _, half, rows, length = volume.shape
    planes = 2 * half
    inner = planes - 2 * EDGE
    width = length // 4 + 2 * SPARE
    axes = ("tm", "space")

    def route(frame_bits, slab_bits):
        return [(f * slabs + s, (f ^ frame_bits) * slabs + (s ^ slab_bits)) for f in range(frames) for s in range(slabs)]

    def swap(value, frame_bits, slab_bits=0):
        return lax.ppermute(value, axes, route(frame_bits, slab_bits))

    def spread(pieces):
        return (pieces[0], swap(pieces[1], 0, 1), swap(pieces[2], 2, 0), swap(pieces[3], 2, 1))

    def halo(side0, side1):
        first = [(s, s ^ 2) for s in range(slabs)]
        second = []
        for s in range(slabs):
            pair = s // 2 + 1 if (s // 2) % 2 else s // 2 - 1
            if 0 <= pair < pairs:
                second.append((s, 2 * pair + s % 2))
        return lax.ppermute(side0, "space", first), lax.ppermute(side1, "space", second)

    side_shape = f32(2, EDGE, rows, width)
    inner_shape = f32(2, inner, rows, width)
    saved_shape = f32(2, 2, SWEEPS - 1, 2, rows, width)
    edges_shape = f32(2, 2, EDGE, rows, width)
    level_scratch = pltpu.VMEM((2, planes, rows, width), jnp.float32)
    packed = pltpu.VMEM((BAND, half, length + LANES), jnp.float32)

    received = swap(volume[0], 1)
    early = call(
        early_kernel, [f32(BAND, half, width)] * 4, warp_coef[0, 1], micros=0.8, scratch=[packed],
    )
    early = spread(early)
    pieces = call(
        first_kernel, [f32(half, rows, width)] * 4, volume[0], received, warp_coef, offsets, thresholds,
        spaces={3: SMEM, 4: SMEM}, micros=4.0, scratch=[pltpu.VMEM((half, rows, length + LANES), jnp.float32)],
    )
    pieces, coeff = lax.optimization_barrier((pieces, early))
    late = call(
        late_kernel, [f32(SECTIONS - 2, BAND, half, width)] * 4, warp_coef, offsets, spaces={1: SMEM}, micros=1.5,
        scratch=[packed],
    )
    mine, near, far = pieces[0], swap(pieces[1], 0, 1), swap(pieces[2], 2, 0)
    last, near, far = lax.optimization_barrier((pieces[3], near, far))
    across = swap(last, 2, 1)
    own, saved = call(
        functools.partial(inner_first_kernel, 0), [inner_shape, saved_shape], mine, near,
        scratch=[level_scratch] * 3, micros=3.5,
    )
    across, own = lax.optimization_barrier((across, own))
    side0, side1 = call(start_kernel, [side_shape, side_shape], mine, near, far, across, micros=0.2)
    late, side0 = lax.optimization_barrier((late, side0))
    halo0, halo1 = halo(side0, side1)
    own, saved = call(
        functools.partial(inner_first_kernel, 1), [inner_shape, saved_shape], far, across, own, saved,
        scratch=[level_scratch] * 3, micros=3.5, aliases={2: 0, 3: 1},
    )
    late = spread(late)
    table = None
    for section in range(1, SECTIONS):
        bit = section % levels
        corners = {1: [(0,)], 2: [(i, 0) for i in range(SECTIONS - 2)]}.get(section, [])
        edges, *shift = call(
            functools.partial(wedge_kernel, corners),
            [edges_shape] + [jax.ShapeDtypeStruct((len(corners), 2, 2), jnp.int32)] * bool(corners),
            side0, side1, halo0, halo1, saved, *({1: (mine, near, far, across), 2: coeff}.get(section, ())),
            smem_outs=(1,), micros=2.4,
        )
        table = shift[0] if shift else table
        partner, partner_edges = own, edges
        if bit != 1:
            partner, partner_edges = lax.optimization_barrier((own, swap(edges, 1 << bit)))
            partner = swap(partner, 1 << bit)
        side0, side1 = call(
            functools.partial(haar_kernel, section, bit), [side_shape, side_shape],
            edges, partner_edges, table, thresholds, *coeff, spaces={2: SMEM, 3: SMEM}, micros=1.1,
            scratch=[pltpu.VMEM((2, 2, EDGE, rows, width), jnp.float32)],
        )
        used = table, thresholds, *coeff
        if section == 1:
            late, side0, side1 = lax.optimization_barrier((late, side0, side1))
            coeff = late
        halo0, halo1 = halo(side0, side1)
        if section == SECTIONS - 1:
            break
        own, saved = call(
            functools.partial(inner_kernel, section, bit), [inner_shape, saved_shape],
            own, partner, side0, side1, *used,
            spaces={4: SMEM, 5: SMEM}, scratch=[level_scratch] * 3, micros=8.0,
        )
    piece_shape = f32(half - EDGE, rows, length // 4)
    edge_shape = f32(EDGE, rows, length // 4)
    slot_saved = f32(2, 1, SWEEPS - 1, 2, rows, width)

    def last_inner(slot):
        return call(
            functools.partial(inner_last_kernel, section, bit, slot), [piece_shape, piece_shape, slot_saved],
            own, partner, side0, side1, *used, spaces={4: SMEM, 5: SMEM}, micros=4.2,
            scratch=[level_scratch] * 3 + [pltpu.VMEM((inner, rows, length // 4), jnp.float32)],
        )

    far, across, saved1 = last_inner(1)
    across = swap(across, 2, 1)
    mine, near, saved0 = last_inner(0)
    across, halo0 = lax.optimization_barrier((across, halo0))
    inners = (mine, swap(near, 0, 1), swap(far, 2, 0), across)
    edges = call(
        wedge_last_kernel, [edge_shape] * 4, side0, side1, halo0, halo1, saved0, saved1, micros=2.5,
        scratch=[pltpu.VMEM((2, 2, EDGE, rows, length // 4), jnp.float32)],
    )
    (out,) = call(output_kernel, [f32(half, rows, length)], *inners, *spread(edges), micros=1.0)
    return out[None]


def solution(mesh):
    return jax.shard_map(
        on_device,
        mesh=mesh,
        in_specs=(
            P("tm", "space", None, None),
            P("tm", None, None, "space", None),
            P("tm", "space", None),
            P(),
        ),
        out_specs=P("tm", "space", None, None),
        check_vma=False,
    )
```

```python
import functools

import jax
import jax.numpy as jnp
from jax import lax
from jax.experimental import pallas as pl
from jax.experimental.pallas import tpu as pltpu
from jax.sharding import PartitionSpec as P

BAND = 4
SECTIONS = 4
SWEEPS = 4
REACH = 6

depth_rate = 0.4
plane_rate = 0.05
root_half = 0.7071067811865476

LANES = 128
HELD = (0.25 / plane_rate) ** 0.5
SPARE = 64
EDGE = SWEEPS
GROUP = {1: 12, 2: 8}
VMEM = pltpu.VMEM
SMEM = pltpu.SMEM


def cells(value):
    return [value[:, i : i + LANES] for i in range(0, value.shape[1], LANES)]


def joined(parts):
    return jnp.concatenate(parts, axis=1)


def lane_ids():
    return lax.broadcasted_iota(jnp.int32, (8, LANES), 1)


def quotient(change):
    return change / (1.0 / plane_rate + change * change)


def moved_right(parts, amount, first):
    turned = [pltpu.roll(part, amount, 1) for part in parts]
    own = lane_ids() >= amount
    ahead = [first] + turned[:-1]
    return [jnp.where(own, a, b) for a, b in zip(turned, ahead)]


def moved_left(parts, amount):
    turned = [pltpu.roll(part, (LANES - amount) % LANES, 1) for part in parts]
    own = lane_ids() < LANES - amount
    return [jnp.where(own, a, b) for a, b in zip(turned, turned[1:])]


def warped_plane(field, coeff_rows, offset):
    width = field.shape[1]
    total = None
    for band_index in range(BAND):
        shifted = pltpu.roll(field, (width + BAND // 2 - band_index - offset) % width, 1)
        term = jnp.broadcast_to(coeff_rows[band_index], shifted.shape) * shifted
        total = term if total is None else total + term
    return total


def haar(own, warped, sign, level, scale):
    value = (own + sign * warped) * scale
    return value - jnp.clip(value, -level, level)


class Sweep:
    def __init__(self, width, edge_first, edge_last, last_lane):
        rows = lax.broadcasted_iota(jnp.int32, (8, width), 0)
        self.inner_rows = rows < 7
        lanes = lane_ids()
        self.first = jnp.where(lanes == SPARE - 1, edge_first, 1.0)
        self.last = jnp.where(lanes == last_lane % LANES, edge_last, 1.0)
        self.last_part = last_lane // LANES

    def depth(self, low, high):
        return quotient(high - low)

    def plane(self, value, flux_below, flux_above):
        width = value.shape[1]
        change = jnp.where(self.inner_rows, pltpu.roll(value, 7, 0) - value, 0.0)
        flux_y = quotient(change)
        change = cells(pltpu.roll(value, width - 1, 1) - value)
        change[0] = change[0] * self.first
        change[self.last_part] = change[self.last_part] * self.last
        flux_x = quotient(joined(change))
        gain = (flux_y - pltpu.roll(flux_y, 1, 0)) + (flux_x - pltpu.roll(flux_x, 1, 1))
        return value + (gain + (depth_rate / plane_rate) * (flux_above - flux_below))


class Place:
    def __init__(self):
        self.tm = lax.axis_index("tm")
        self.space = lax.axis_index("space")
        self.pairs = lax.axis_size("space") // 2
        self.far = (self.tm // 2) % 2
        self.slab = self.space % 2
        self.chunk = 2 * self.far + self.slab
        self.pair = self.space // 2
        self.odd = self.pair % 2

    def lower(self, slot, bit):
        value = (self.tm // (1 << bit)) % 2
        if bit == 1 and slot == 1:
            value = 1 - value
        return value == 0

    def signs(self, slot, bit, level):
        is_lower = self.lower(slot, bit)
        sign = jnp.where(is_lower, 1.0, -1.0).astype(jnp.float32)
        return sign, jnp.where(is_lower, 0.0, HELD * level).astype(jnp.float32)

    def sweep(self, width):
        first = jnp.where(self.chunk == 0, 0.0, 1.0).astype(jnp.float32)
        last = jnp.where(self.chunk == 3, 0.0, 1.0).astype(jnp.float32)
        return Sweep(width, first, last, width - SPARE - 1)

    def spot(self, side, distance, planes):
        is_top = self.odd == side
        return jnp.where(is_top, planes - 1 - distance, distance)

    def open_face(self, side):
        if side == 0:
            return jnp.float32(1.0)
        closed = (self.pair == 0) | (self.pair == self.pairs - 1)
        return jnp.where(closed, 0.0, 1.0).astype(jnp.float32)


def call(body, outs, *args, spaces=None, scratch=(), micros=1.0, smem_outs=(), aliases=None, room=40):
    spaces = spaces or {}
    in_specs = [pl.BlockSpec(memory_space=spaces.get(i, VMEM)) for i in range(len(args))]
    out_specs = [pl.BlockSpec(memory_space=SMEM if i in smem_outs else VMEM) for i in range(len(outs))]
    moved = sum(a.size * 4 for a in args) + sum(o.size * 4 for o in outs)
    return pl.pallas_call(
        body,
        out_shape=outs,
        in_specs=in_specs,
        out_specs=out_specs,
        scratch_shapes=list(scratch),
        input_output_aliases=aliases or {},
        compiler_params=pltpu.CompilerParams(vmem_limit_bytes=room << 20),
        cost_estimate=pl.CostEstimate(flops=int(micros * 1.1e9), bytes_accessed=int(moved), transcendentals=0),
    )(*args)


def f32(*shape):
    return jax.ShapeDtypeStruct(shape, jnp.float32)


def marked(value, offset):
    return jnp.where(lane_ids() == 0, offset.astype(jnp.float32), value)


def pack_section(place, coeff_ref, whole, outs):
    planes, width = coeff_ref.shape[1:]
    step = width // 4
    zero = jnp.zeros((8, LANES), jnp.float32)
    for k in range(BAND):
        for z in range(0, planes, 8):
            value = coeff_ref[k, z : z + 8, :]
            whole[k, z : z + 8] = joined(moved_right(cells(value) + [zero], SPARE, zero))
    for number, out_ref in enumerate(outs):
        start = pl.multiple_of((place.chunk ^ number) * step, LANES)
        out_ref[...] = whole[:, :, pl.ds(start, step + LANES)]


def early_kernel(coeff_ref, *refs):
    pack_section(Place(), coeff_ref, refs[4], refs[:4])


def late_kernel(coeff_ref, offset_ref, *refs):
    for section in range(2, SECTIONS):
        outs = [ref.at[section - 2] for ref in refs[:4]]
        pack_section(Place(), coeff_ref.at[0, section], refs[4], outs)
        for out in outs:
            out[0, 0:8, 0:LANES] = marked(out[0, 0:8, 0:LANES], offset_ref[0, 0, section])


def first_kernel(own_ref, partner_ref, coeff_ref, offset_ref, level_ref, *refs):
    out_refs, whole = refs[:4], refs[4]
    planes, _, width = own_ref.shape
    place = Place()
    sign, level = place.signs(0, 0, level_ref[0])
    offset = offset_ref[0, 0, 0]
    step = width // 4
    zero = jnp.zeros((8, LANES), jnp.float32)
    no_rows = jnp.zeros((1, LANES), jnp.float32)

    def body(z, carry):
        field = joined([partner_ref[z], zero])
        width = field.shape[1]
        shifted = pltpu.roll(field, (width + BAND // 2 - offset) % width, 1)
        warped = None
        for k in range(BAND):
            row = joined([coeff_ref[0, 0, k, pl.ds(z, 1), :], no_rows])
            term = jnp.broadcast_to(row, shifted.shape) * (pltpu.roll(shifted, width - k, 1) if k else shifted)
            warped = term if warped is None else warped + term
        value = haar(joined([own_ref[z], zero]), warped, sign, level, HELD * root_half)
        whole[z] = pltpu.roll(value, SPARE, 1)
        return carry

    lax.fori_loop(0, planes, body, 0, unroll=2)
    for number, out_ref in enumerate(out_refs):
        start = pl.multiple_of((place.chunk ^ number) * step, LANES)
        out_ref[...] = whole[:, :, pl.ds(start, step + LANES)]
        out_ref[0, :, 0:LANES] = marked(out_ref[0, :, 0:LANES], offset_ref[0, 0, 1])


def coeff_rows(section, refs):
    if section == 1:
        return [lambda k, z, ref=ref: ref[k, pl.ds(z, 1), :] for ref in refs]
    return [lambda k, z, ref=ref: ref[section - 2, k, pl.ds(z, 1), :] for ref in refs]


def start_kernel(self_ref, near_ref, far_ref, across_ref, side0_ref, side1_ref):
    place = Place()
    half = self_ref.shape[0]
    for side, out_ref in enumerate((side0_ref, side1_ref)):
        is_top = place.odd == side
        slab = jnp.where(is_top, 1, 0)
        for own_slab in (True, False):
            pieces = (self_ref, far_ref) if own_slab else (near_ref, across_ref)

            @pl.when((slab == place.slab) == own_slab)
            def _():
                for slot, piece in enumerate(pieces):
                    for e in range(EDGE):
                        out_ref[slot, e] = piece[jnp.where(is_top, half - 1 - e, e)]


def trapezoid(place, load, planes, emit, saved_ref, one, two, slots=(0, 1)):
    width = one.shape[-1]
    sweep = place.sweep(width)
    size = GROUP[len(slots)]
    for level in range(1, SWEEPS + 1):
        def source(slot, p, level=level):
            if level == 1:
                return load(slot, p)
            return (one, two)[level % 2][slot, p]

        def put(slot, p, value, level=level):
            if level == SWEEPS:
                emit(slot, p - EDGE, value)
            else:
                (two, one)[level % 2][slot, p] = value

        carry = []
        for slot in slots:
            low, here = source(slot, level - 1), source(slot, level)
            carry += [here, sweep.depth(low, here)]

        def body(i, carry):
            return step(i, carry, size)

        def step(i, carry, group):
            new = []
            for slot in slots:
                at = 2 * slots.index(slot)
                here, below = carry[at : at + 2]
                for j in range(group):
                    p = level + size * i + j
                    high = source(slot, p + 1)
                    above = sweep.depth(here, high)
                    put(slot, p, sweep.plane(here, below, above))
                    here, below = high, above
                new += [here, below]
            return new

        count = planes - 2 * level
        carry = lax.fori_loop(0, count // size, body, carry)
        if count % size:
            step(count // size, carry, count % size)
        if level < SWEEPS:
            kept = (two, one)[level % 2]
            for slot in slots:
                for side in range(2):
                    for j in range(2):
                        spot = place.spot(side, level + j, planes)
                        saved_ref[side, slot % saved_ref.shape[1], level - 1, j] = kept[slot, spot]


def inner_first_kernel(slot, own_ref, other_ref, *refs):
    out_ref, saved_ref, state, one, two = refs[-5:]
    place = Place()
    half = own_ref.shape[0]
    state[slot, pl.ds(place.slab * half, half)] = own_ref[...]
    state[slot, pl.ds((1 - place.slab) * half, half)] = other_ref[...]

    def emit(slot, i, value):
        out_ref[slot, i] = value

    trapezoid(place, lambda slot, p: state[slot, p], 2 * half, emit, saved_ref, one, two, (slot,))


def finished(value):
    return (1.0 / HELD) * joined(moved_left(cells(value), SPARE)[: (value.shape[1] - 2 * SPARE) // LANES])


def inner_haar(place, section, bit, slots, own_ref, partner_ref, sides, coeff_refs, offset_ref, level_ref, zero_level):
    inner = own_ref.shape[1]
    planes = inner + 2 * EDGE
    half = planes // 2
    rows_of = coeff_rows(section, coeff_refs)
    for slot in slots:
        for side, ref in enumerate(sides):
            for e in range(EDGE):
                zero_level[slot, place.spot(side, e, planes)] = ref[slot, e]
    for slot in slots:
        sign, level = place.signs(slot, bit, level_ref[section])
        other = 1 - slot if bit == 1 else slot
        for away in range(2):
            slab = place.slab ^ away
            offset = offset_ref[0 if section == 1 else section - 2, slot, away]
            start = jnp.where(slab == 0, EDGE, 0)
            for i in range(half - EDGE):
                z = start + i
                p = slab * half + z
                rows = [rows_of[2 * slot + away](k, z) for k in range(BAND)]
                warped = warped_plane(partner_ref[other, p - EDGE], rows, offset)
                zero_level[slot, p] = haar(own_ref[slot, p - EDGE], warped, sign, level, root_half)


def inner_kernel(section, bit, own_ref, partner_ref, side0_ref, side1_ref, offset_ref, level_ref, *refs):
    coeff_refs, (out_ref, saved_ref, zero_level, one, two) = refs[:4], refs[4:]
    place = Place()
    planes = own_ref.shape[1] + 2 * EDGE
    sides = (side0_ref, side1_ref)
    inner_haar(place, section, bit, (0, 1), own_ref, partner_ref, sides, coeff_refs, offset_ref, level_ref, zero_level)

    def emit(slot, i, value):
        out_ref[slot, i] = value

    trapezoid(place, lambda slot, p: zero_level[slot, p], planes, emit, saved_ref, one, two)


def inner_last_kernel(section, bit, slot, own_ref, partner_ref, side0_ref, side1_ref, offset_ref, level_ref, *refs):
    coeff_refs, (mine_ref, other_ref, saved_ref, zero_level, one, two, done) = refs[:4], refs[4:]
    place = Place()
    planes = own_ref.shape[1] + 2 * EDGE
    sides = (side0_ref, side1_ref)
    inner_haar(place, section, bit, (slot,), own_ref, partner_ref, sides, coeff_refs, offset_ref, level_ref, zero_level)

    def emit(slot, i, value):
        done[i] = finished(value)

    trapezoid(place, lambda slot, p: zero_level[slot, p], planes, emit, saved_ref, one, two, (slot,))
    count = mine_ref.shape[0]
    mine_ref[...] = done[pl.ds(place.slab * count, count)]
    other_ref[...] = done[pl.ds((1 - place.slab) * count, count)]


def wedge(place, sweep, side, edge_ref, halo_ref, saved):
    open_face = place.open_face(side)
    values = [
        [halo_ref[slot, h] for h in (3, 2, 1, 0)] + [edge_ref[slot, 0], edge_ref[slot, 1]] for slot in range(2)
    ]
    for level in range(1, SWEEPS + 1):
        for slot in range(2):
            here = values[slot]
            fluxes = [sweep.depth(a, b) for a, b in zip(here[:-1], here[1:])]
            fluxes[EDGE - level] = fluxes[EDGE - level] * open_face
            here = [sweep.plane(here[i], fluxes[i - 1], fluxes[i]) for i in range(1, 5)]
            if level < SWEEPS:
                here += [saved(side, slot, level - 1, j) for j in range(2)]
            values[slot] = here
    return values


def wedge_kernel(corners, side0_ref, side1_ref, halo0_ref, halo1_ref, saved_ref, *refs):
    marked_refs, out_ref = refs[: 4 * bool(corners)], refs[4 * bool(corners)]
    place = Place()
    sweep = place.sweep(side0_ref.shape[-1])
    for number, ref in enumerate(marked_refs):
        for i, at in enumerate(corners):
            value = jnp.max(jnp.where(lane_ids() == 0, ref[*at, 0:8, 0:LANES], -100.0))
            refs[5][i, number // 2, number % 2] = value.astype(jnp.int32)
    for side, (edge, halo) in enumerate(((side0_ref, halo0_ref), (side1_ref, halo1_ref))):
        values = wedge(place, sweep, side, edge, halo, lambda *at: saved_ref[at])
        for slot in range(2):
            for e in range(EDGE):
                out_ref[side, slot, e] = values[slot][e]


def haar_kernel(section, bit, own_ref, partner_ref, offset_ref, level_ref, *refs):
    coeff_refs, (out0_ref, out1_ref, done) = refs[:4], refs[4:]
    place = Place()
    half = coeff_refs[0].shape[-2]
    rows_of = coeff_rows(section, coeff_refs)
    for slot in range(2):
        sign, level = place.signs(slot, bit, level_ref[section])
        other = 1 - slot if bit == 1 else slot
        for away in range(2):
            is_top = place.slab ^ away == 1
            side = jnp.where(is_top, place.odd, 1 - place.odd)
            offset = offset_ref[0 if section == 1 else section - 2, slot, away]
            for e in range(EDGE):
                z = jnp.where(is_top, half - 1 - e, e)
                rows = [rows_of[2 * slot + away](k, z) for k in range(BAND)]
                warped = warped_plane(partner_ref[side, other, e], rows, offset)
                done[side, slot, e] = haar(own_ref[side, slot, e], warped, sign, level, root_half)
    out0_ref[...] = done[0]
    out1_ref[...] = done[1]


def wedge_last_kernel(side0_ref, side1_ref, halo0_ref, halo1_ref, saved0_ref, saved1_ref, *refs):
    out_refs, done = refs[:4], refs[4]
    place = Place()
    sweep = place.sweep(side0_ref.shape[-1])
    saved_refs = (saved0_ref, saved1_ref)

    def saved(side, slot, level, j):
        return saved_refs[slot][side, 0, level, j]

    for side, (edge, halo) in enumerate(((side0_ref, halo0_ref), (side1_ref, halo1_ref))):
        values = wedge(place, sweep, side, edge, halo, saved)
        for slot in range(2):
            for e in range(EDGE):
                done[side, slot, e] = finished(values[slot][e])
    for number, out_ref in enumerate(out_refs):
        slab = place.slab ^ (number % 2)
        side = jnp.where(slab == 1, place.odd, 1 - place.odd)
        out_ref[...] = done[side, number // 2]


def output_kernel(*refs):
    inner_refs, edge_refs, out_ref = refs[:4], refs[4:8], refs[8]
    place = Place()
    half = out_ref.shape[0]
    inner, _, step = inner_refs[0].shape
    for number in range(4):
        lanes = pl.ds(pl.multiple_of((place.chunk ^ number) * step, LANES), step)
        out_ref[pl.ds((1 - place.slab) * EDGE, inner), :, lanes] = inner_refs[number][...]
        for e in range(EDGE):
            out_ref[jnp.where(place.slab == 1, half - 1 - e, e), :, lanes] = edge_refs[number][e]


def on_device(volume, warp_coef, offsets, thresholds):
    frames, slabs = lax.axis_size("tm"), lax.axis_size("space")
    levels = frames.bit_length() - 1
    pairs = slabs // 2
    _, half, rows, length = volume.shape
    planes = 2 * half
    inner = planes - 2 * EDGE
    width = length // 4 + 2 * SPARE
    axes = ("tm", "space")

    def route(frame_bits, slab_bits):
        return [(f * slabs + s, (f ^ frame_bits) * slabs + (s ^ slab_bits)) for f in range(frames) for s in range(slabs)]

    def swap(value, frame_bits, slab_bits=0):
        return lax.ppermute(value, axes, route(frame_bits, slab_bits))

    def spread(pieces):
        return (pieces[0], swap(pieces[1], 0, 1), swap(pieces[2], 2, 0), swap(pieces[3], 2, 1))

    def halo(side0, side1):
        first = [(s, s ^ 2) for s in range(slabs)]
        second = []
        for s in range(slabs):
            pair = s // 2 + 1 if (s // 2) % 2 else s // 2 - 1
            if 0 <= pair < pairs:
                second.append((s, 2 * pair + s % 2))
        return lax.ppermute(side0, "space", first), lax.ppermute(side1, "space", second)

    side_shape = f32(2, EDGE, rows, width)
    inner_shape = f32(2, inner, rows, width)
    saved_shape = f32(2, 2, SWEEPS - 1, 2, rows, width)
    edges_shape = f32(2, 2, EDGE, rows, width)
    level_scratch = pltpu.VMEM((2, planes, rows, width), jnp.float32)
    packed = pltpu.VMEM((BAND, half, length + LANES), jnp.float32)

    received = swap(volume[0], 1)
    early = call(
        early_kernel, [f32(BAND, half, width)] * 4, warp_coef[0, 1], micros=0.8, scratch=[packed],
    )
    early = spread(early)
    pieces = call(
        first_kernel, [f32(half, rows, width)] * 4, volume[0], received, warp_coef, offsets, thresholds,
        spaces={3: SMEM, 4: SMEM}, micros=4.0, scratch=[pltpu.VMEM((half, rows, length + LANES), jnp.float32)],
    )
    pieces, coeff = lax.optimization_barrier((pieces, early))
    late = call(
        late_kernel, [f32(SECTIONS - 2, BAND, half, width)] * 4, warp_coef, offsets, spaces={1: SMEM}, micros=1.5,
        scratch=[packed],
    )
    mine, near, far = pieces[0], swap(pieces[1], 0, 1), swap(pieces[2], 2, 0)
    last, near, far = lax.optimization_barrier((pieces[3], near, far))
    across = swap(last, 2, 1)
    own, saved = call(
        functools.partial(inner_first_kernel, 0), [inner_shape, saved_shape], mine, near,
        scratch=[level_scratch] * 3, micros=3.5,
    )
    across, own = lax.optimization_barrier((across, own))
    side0, side1 = call(start_kernel, [side_shape, side_shape], mine, near, far, across, micros=0.2)
    late, side0 = lax.optimization_barrier((late, side0))
    halo0, halo1 = halo(side0, side1)
    own, saved = call(
        functools.partial(inner_first_kernel, 1), [inner_shape, saved_shape], far, across, own, saved,
        scratch=[level_scratch] * 3, micros=3.5, aliases={2: 0, 3: 1},
    )
    late = spread(late)
    table = None
    for section in range(1, SECTIONS):
        bit = section % levels
        corners = {1: [(0,)], 2: [(i, 0) for i in range(SECTIONS - 2)]}.get(section, [])
        edges, *shift = call(
            functools.partial(wedge_kernel, corners),
            [edges_shape] + [jax.ShapeDtypeStruct((len(corners), 2, 2), jnp.int32)] * bool(corners),
            side0, side1, halo0, halo1, saved, *({1: (mine, near, far, across), 2: coeff}.get(section, ())),
            smem_outs=(1,), micros=2.4,
        )
        table = shift[0] if shift else table
        partner, partner_edges = own, edges
        if bit != 1:
            partner, partner_edges = lax.optimization_barrier((own, swap(edges, 1 << bit)))
            partner = swap(partner, 1 << bit)
        side0, side1 = call(
            functools.partial(haar_kernel, section, bit), [side_shape, side_shape],
            edges, partner_edges, table, thresholds, *coeff, spaces={2: SMEM, 3: SMEM}, micros=1.1,
            scratch=[pltpu.VMEM((2, 2, EDGE, rows, width), jnp.float32)],
        )
        used = table, thresholds, *coeff
        if section == 1:
            late, own = lax.optimization_barrier((late, own))
            partner = own
            coeff = late
        halo0, halo1 = halo(side0, side1)
        if section == SECTIONS - 1:
            break
        own, saved = call(
            functools.partial(inner_kernel, section, bit), [inner_shape, saved_shape],
            own, partner, side0, side1, *used,
            spaces={4: SMEM, 5: SMEM}, scratch=[level_scratch] * 3, micros=8.0,
        )
    piece_shape = f32(half - EDGE, rows, length // 4)
    edge_shape = f32(EDGE, rows, length // 4)
    slot_saved = f32(2, 1, SWEEPS - 1, 2, rows, width)

    def last_inner(slot):
        return call(
            functools.partial(inner_last_kernel, section, bit, slot), [piece_shape, piece_shape, slot_saved],
            own, partner, side0, side1, *used, spaces={4: SMEM, 5: SMEM}, micros=4.2,
            scratch=[level_scratch] * 3 + [pltpu.VMEM((inner, rows, length // 4), jnp.float32)],
        )

    far, across, saved1 = last_inner(1)
    across = swap(across, 2, 1)
    mine, near, saved0 = last_inner(0)
    across, halo0 = lax.optimization_barrier((across, halo0))
    inners = (mine, swap(near, 0, 1), swap(far, 2, 0), across)
    edges = call(
        wedge_last_kernel, [edge_shape] * 4, side0, side1, halo0, halo1, saved0, saved1, micros=2.5,
        scratch=[pltpu.VMEM((2, 2, EDGE, rows, length // 4), jnp.float32)],
    )
    (out,) = call(output_kernel, [f32(half, rows, length)], *inners, *spread(edges), micros=1.0)
    return out[None]


def solution(mesh):
    return jax.shard_map(
        on_device,
        mesh=mesh,
        in_specs=(
            P("tm", "space", None, None),
            P("tm", None, None, "space", None),
            P("tm", "space", None),
            P(),
        ),
        out_specs=P("tm", "space", None, None),
        check_vma=False,
    )
```

```python
import functools

import jax
import jax.numpy as jnp
from jax import lax
from jax.experimental import pallas as pl
from jax.experimental.pallas import tpu as pltpu
from jax.sharding import PartitionSpec as P

BAND = 4
SECTIONS = 4
SWEEPS = 4
REACH = 6

depth_rate = 0.4
plane_rate = 0.05
root_half = 0.7071067811865476

LANES = 128
HELD = (0.25 / plane_rate) ** 0.5
SPARE = 64
EDGE = SWEEPS
GROUP = {1: 12, 2: 8}
VMEM = pltpu.VMEM
SMEM = pltpu.SMEM


def cells(value):
    return [value[:, i : i + LANES] for i in range(0, value.shape[1], LANES)]


def joined(parts):
    return jnp.concatenate(parts, axis=1)


def lane_ids():
    return lax.broadcasted_iota(jnp.int32, (8, LANES), 1)


def quotient(change):
    return change / (1.0 / plane_rate + change * change)


def moved_right(parts, amount, first):
    turned = [pltpu.roll(part, amount, 1) for part in parts]
    own = lane_ids() >= amount
    ahead = [first] + turned[:-1]
    return [jnp.where(own, a, b) for a, b in zip(turned, ahead)]


def moved_left(parts, amount):
    turned = [pltpu.roll(part, (LANES - amount) % LANES, 1) for part in parts]
    own = lane_ids() < LANES - amount
    return [jnp.where(own, a, b) for a, b in zip(turned, turned[1:])]


def warped_plane(field, coeff_rows, offset):
    width = field.shape[1]
    total = None
    for band_index in range(BAND):
        shifted = pltpu.roll(field, (width + BAND // 2 - band_index - offset) % width, 1)
        term = jnp.broadcast_to(coeff_rows[band_index], shifted.shape) * shifted
        total = term if total is None else total + term
    return total


def haar(own, warped, sign, level, scale):
    value = (own + sign * warped) * scale
    return value - jnp.clip(value, -level, level)


class Sweep:
    def __init__(self, width, edge_first, edge_last, last_lane):
        rows = lax.broadcasted_iota(jnp.int32, (8, width), 0)
        self.inner_rows = rows < 7
        lanes = lane_ids()
        self.first = jnp.where(lanes == SPARE - 1, edge_first, 1.0)
        self.last = jnp.where(lanes == last_lane % LANES, edge_last, 1.0)
        self.last_part = last_lane // LANES

    def depth(self, low, high):
        return quotient(high - low)

    def plane(self, value, flux_below, flux_above):
        width = value.shape[1]
        change = jnp.where(self.inner_rows, pltpu.roll(value, 7, 0) - value, 0.0)
        flux_y = quotient(change)
        change = cells(pltpu.roll(value, width - 1, 1) - value)
        change[0] = change[0] * self.first
        change[self.last_part] = change[self.last_part] * self.last
        flux_x = quotient(joined(change))
        gain = (flux_y - pltpu.roll(flux_y, 1, 0)) + (flux_x - pltpu.roll(flux_x, 1, 1))
        return value + (gain + (depth_rate / plane_rate) * (flux_above - flux_below))


class Place:
    def __init__(self):
        self.tm = lax.axis_index("tm")
        self.space = lax.axis_index("space")
        self.pairs = lax.axis_size("space") // 2
        self.far = (self.tm // 2) % 2
        self.slab = self.space % 2
        self.chunk = 2 * self.far + self.slab
        self.pair = self.space // 2
        self.odd = self.pair % 2

    def lower(self, slot, bit):
        value = (self.tm // (1 << bit)) % 2
        if bit == 1 and slot == 1:
            value = 1 - value
        return value == 0

    def signs(self, slot, bit, level):
        is_lower = self.lower(slot, bit)
        sign = jnp.where(is_lower, 1.0, -1.0).astype(jnp.float32)
        return sign, jnp.where(is_lower, 0.0, HELD * level).astype(jnp.float32)

    def sweep(self, width):
        first = jnp.where(self.chunk == 0, 0.0, 1.0).astype(jnp.float32)
        last = jnp.where(self.chunk == 3, 0.0, 1.0).astype(jnp.float32)
        return Sweep(width, first, last, width - SPARE - 1)

    def spot(self, side, distance, planes):
        is_top = self.odd == side
        return jnp.where(is_top, planes - 1 - distance, distance)

    def open_face(self, side):
        if side == 0:
            return jnp.float32(1.0)
        closed = (self.pair == 0) | (self.pair == self.pairs - 1)
        return jnp.where(closed, 0.0, 1.0).astype(jnp.float32)


def call(body, outs, *args, spaces=None, scratch=(), micros=1.0, smem_outs=(), aliases=None, room=40):
    spaces = spaces or {}
    in_specs = [pl.BlockSpec(memory_space=spaces.get(i, VMEM)) for i in range(len(args))]
    out_specs = [pl.BlockSpec(memory_space=SMEM if i in smem_outs else VMEM) for i in range(len(outs))]
    moved = sum(a.size * 4 for a in args) + sum(o.size * 4 for o in outs)
    return pl.pallas_call(
        body,
        out_shape=outs,
        in_specs=in_specs,
        out_specs=out_specs,
        scratch_shapes=list(scratch),
        input_output_aliases=aliases or {},
        compiler_params=pltpu.CompilerParams(vmem_limit_bytes=room << 20),
        cost_estimate=pl.CostEstimate(flops=int(micros * 1.1e9), bytes_accessed=int(moved), transcendentals=0),
    )(*args)


def f32(*shape):
    return jax.ShapeDtypeStruct(shape, jnp.float32)


def marked(value, offset):
    return jnp.where(lane_ids() == 0, offset.astype(jnp.float32), value)


def pack_section(place, coeff_ref, whole, outs):
    planes, width = coeff_ref.shape[1:]
    step = width // 4
    zero = jnp.zeros((8, LANES), jnp.float32)
    for k in range(BAND):
        for z in range(0, planes, 8):
            value = coeff_ref[k, z : z + 8, :]
            whole[k, z : z + 8] = joined(moved_right(cells(value) + [zero], SPARE, zero))
    for number, out_ref in enumerate(outs):
        start = pl.multiple_of((place.chunk ^ number) * step, LANES)
        out_ref[...] = whole[:, :, pl.ds(start, step + LANES)]


def early_kernel(coeff_ref, *refs):
    pack_section(Place(), coeff_ref, refs[4], refs[:4])


def late_kernel(coeff_ref, offset_ref, *refs):
    for section in range(2, SECTIONS):
        outs = [ref.at[section - 2] for ref in refs[:4]]
        pack_section(Place(), coeff_ref.at[0, section], refs[4], outs)
        for out in outs:
            out[0, 0:8, 0:LANES] = marked(out[0, 0:8, 0:LANES], offset_ref[0, 0, section])


def first_kernel(own_ref, partner_ref, coeff_ref, offset_ref, level_ref, *refs):
    out_refs, whole = refs[:4], refs[4]
    planes, _, width = own_ref.shape
    place = Place()
    sign, level = place.signs(0, 0, level_ref[0])
    offset = offset_ref[0, 0, 0]
    step = width // 4
    zero = jnp.zeros((8, LANES), jnp.float32)
    no_rows = jnp.zeros((1, LANES), jnp.float32)

    def body(z, carry):
        field = joined([partner_ref[z], zero])
        width = field.shape[1]
        shifted = pltpu.roll(field, (width + BAND // 2 - offset) % width, 1)
        warped = None
        for k in range(BAND):
            row = joined([coeff_ref[0, 0, k, pl.ds(z, 1), :], no_rows])
            term = jnp.broadcast_to(row, shifted.shape) * (pltpu.roll(shifted, width - k, 1) if k else shifted)
            warped = term if warped is None else warped + term
        value = haar(joined([own_ref[z], zero]), warped, sign, level, HELD * root_half)
        whole[z] = pltpu.roll(value, SPARE, 1)
        return carry

    lax.fori_loop(0, planes, body, 0, unroll=2)
    for number, out_ref in enumerate(out_refs):
        start = pl.multiple_of((place.chunk ^ number) * step, LANES)
        out_ref[...] = whole[:, :, pl.ds(start, step + LANES)]
        out_ref[0, :, 0:LANES] = marked(out_ref[0, :, 0:LANES], offset_ref[0, 0, 1])


def coeff_rows(section, refs):
    if section == 1:
        return [lambda k, z, ref=ref: ref[k, pl.ds(z, 1), :] for ref in refs]
    return [lambda k, z, ref=ref: ref[section - 2, k, pl.ds(z, 1), :] for ref in refs]


def start_kernel(self_ref, near_ref, far_ref, across_ref, side0_ref, side1_ref):
    place = Place()
    half = self_ref.shape[0]
    for side, out_ref in enumerate((side0_ref, side1_ref)):
        is_top = place.odd == side
        slab = jnp.where(is_top, 1, 0)
        for own_slab in (True, False):
            pieces = (self_ref, far_ref) if own_slab else (near_ref, across_ref)

            @pl.when((slab == place.slab) == own_slab)
            def _():
                for slot, piece in enumerate(pieces):
                    for e in range(EDGE):
                        out_ref[slot, e] = piece[jnp.where(is_top, half - 1 - e, e)]


def trapezoid(place, load, planes, emit, saved_ref, one, two, slots=(0, 1)):
    width = one.shape[-1]
    sweep = place.sweep(width)
    size = GROUP[len(slots)]
    for level in range(1, SWEEPS + 1):
        def source(slot, p, level=level):
            if level == 1:
                return load(slot, p)
            return (one, two)[level % 2][slot, p]

        def put(slot, p, value, level=level):
            if level == SWEEPS:
                emit(slot, p - EDGE, value)
            else:
                (two, one)[level % 2][slot, p] = value

        carry = []
        for slot in slots:
            low, here = source(slot, level - 1), source(slot, level)
            carry += [here, sweep.depth(low, here)]

        def body(i, carry):
            return step(i, carry, size)

        def step(i, carry, group):
            new = []
            for slot in slots:
                at = 2 * slots.index(slot)
                here, below = carry[at : at + 2]
                for j in range(group):
                    p = level + size * i + j
                    high = source(slot, p + 1)
                    above = sweep.depth(here, high)
                    put(slot, p, sweep.plane(here, below, above))
                    here, below = high, above
                new += [here, below]
            return new

        count = planes - 2 * level
        carry = lax.fori_loop(0, count // size, body, carry)
        if count % size:
            step(count // size, carry, count % size)
        if level < SWEEPS:
            kept = (two, one)[level % 2]
            for slot in slots:
                for side in range(2):
                    for j in range(2):
                        spot = place.spot(side, level + j, planes)
                        saved_ref[side, slot % saved_ref.shape[1], level - 1, j] = kept[slot, spot]


def inner_first_kernel(slot, own_ref, other_ref, *refs):
    out_ref, saved_ref, state, one, two = refs[-5:]
    place = Place()
    half = own_ref.shape[0]
    state[slot, pl.ds(place.slab * half, half)] = own_ref[...]
    state[slot, pl.ds((1 - place.slab) * half, half)] = other_ref[...]

    def emit(slot, i, value):
        out_ref[slot, i] = value

    trapezoid(place, lambda slot, p: state[slot, p], 2 * half, emit, saved_ref, one, two, (slot,))


def finished(value):
    return (1.0 / HELD) * joined(moved_left(cells(value), SPARE)[: (value.shape[1] - 2 * SPARE) // LANES])


def inner_haar(place, section, bit, slots, own_ref, partner_ref, sides, coeff_refs, offset_ref, level_ref, zero_level):
    inner = own_ref.shape[1]
    planes = inner + 2 * EDGE
    half = planes // 2
    rows_of = coeff_rows(section, coeff_refs)
    for slot in slots:
        for side, ref in enumerate(sides):
            for e in range(EDGE):
                zero_level[slot, place.spot(side, e, planes)] = ref[slot, e]
    for slot in slots:
        sign, level = place.signs(slot, bit, level_ref[section])
        other = 1 - slot if bit == 1 else slot
        for away in range(2):
            slab = place.slab ^ away
            offset = offset_ref[0, slot, away]
            start = jnp.where(slab == 0, EDGE, 0)
            for i in range(half - EDGE):
                z = start + i
                p = slab * half + z
                rows = [rows_of[2 * slot + away](k, z) for k in range(BAND)]
                warped = warped_plane(partner_ref[other, p - EDGE], rows, offset)
                zero_level[slot, p] = haar(own_ref[slot, p - EDGE], warped, sign, level, root_half)


def inner_kernel(section, bit, own_ref, partner_ref, side0_ref, side1_ref, offset_ref, level_ref, *refs):
    coeff_refs, (out_ref, saved_ref, zero_level, one, two) = refs[:4], refs[4:]
    place = Place()
    planes = own_ref.shape[1] + 2 * EDGE
    sides = (side0_ref, side1_ref)
    inner_haar(place, section, bit, (0, 1), own_ref, partner_ref, sides, coeff_refs, offset_ref, level_ref, zero_level)

    def emit(slot, i, value):
        out_ref[slot, i] = value

    trapezoid(place, lambda slot, p: zero_level[slot, p], planes, emit, saved_ref, one, two)


def inner_last_kernel(section, bit, slot, own_ref, partner_ref, side0_ref, side1_ref, offset_ref, level_ref, *refs):
    coeff_refs, (mine_ref, other_ref, saved_ref, zero_level, one, two, done) = refs[:4], refs[4:]
    place = Place()
    planes = own_ref.shape[1] + 2 * EDGE
    sides = (side0_ref, side1_ref)
    inner_haar(place, section, bit, (slot,), own_ref, partner_ref, sides, coeff_refs, offset_ref, level_ref, zero_level)

    def emit(slot, i, value):
        done[i] = finished(value)

    trapezoid(place, lambda slot, p: zero_level[slot, p], planes, emit, saved_ref, one, two, (slot,))
    count = mine_ref.shape[0]
    mine_ref[...] = done[pl.ds(place.slab * count, count)]
    other_ref[...] = done[pl.ds((1 - place.slab) * count, count)]


def wedge(place, sweep, side, edge_ref, halo_ref, saved):
    open_face = place.open_face(side)
    values = [
        [halo_ref[slot, h] for h in (3, 2, 1, 0)] + [edge_ref[slot, 0], edge_ref[slot, 1]] for slot in range(2)
    ]
    for level in range(1, SWEEPS + 1):
        for slot in range(2):
            here = values[slot]
            fluxes = [sweep.depth(a, b) for a, b in zip(here[:-1], here[1:])]
            fluxes[EDGE - level] = fluxes[EDGE - level] * open_face
            here = [sweep.plane(here[i], fluxes[i - 1], fluxes[i]) for i in range(1, 5)]
            if level < SWEEPS:
                here += [saved(side, slot, level - 1, j) for j in range(2)]
            values[slot] = here
    return values


def wedge_kernel(corners, side0_ref, side1_ref, halo0_ref, halo1_ref, saved_ref, *refs):
    marked_refs, out_ref = refs[: 4 * bool(corners)], refs[4 * bool(corners)]
    place = Place()
    sweep = place.sweep(side0_ref.shape[-1])
    for number, ref in enumerate(marked_refs):
        for i, at in enumerate(corners):
            value = jnp.max(jnp.where(lane_ids() == 0, ref[*at, 0:8, 0:LANES], -100.0))
            refs[5][i, number // 2, number % 2] = value.astype(jnp.int32)
    for side, (edge, halo) in enumerate(((side0_ref, halo0_ref), (side1_ref, halo1_ref))):
        values = wedge(place, sweep, side, edge, halo, lambda *at: saved_ref[at])
        for slot in range(2):
            for e in range(EDGE):
                out_ref[side, slot, e] = values[slot][e]


def haar_kernel(section, bit, own_ref, partner_ref, offset_ref, level_ref, *refs):
    coeff_refs, (out0_ref, out1_ref, done) = refs[:4], refs[4:]
    place = Place()
    half = coeff_refs[0].shape[-2]
    rows_of = coeff_rows(section, coeff_refs)
    for slot in range(2):
        sign, level = place.signs(slot, bit, level_ref[section])
        other = 1 - slot if bit == 1 else slot
        for away in range(2):
            is_top = place.slab ^ away == 1
            side = jnp.where(is_top, place.odd, 1 - place.odd)
            offset = offset_ref[0, slot, away]
            for e in range(EDGE):
                z = jnp.where(is_top, half - 1 - e, e)
                rows = [rows_of[2 * slot + away](k, z) for k in range(BAND)]
                warped = warped_plane(partner_ref[side, other, e], rows, offset)
                done[side, slot, e] = haar(own_ref[side, slot, e], warped, sign, level, root_half)
    out0_ref[...] = done[0]
    out1_ref[...] = done[1]


def wedge_last_kernel(side0_ref, side1_ref, halo0_ref, halo1_ref, saved0_ref, saved1_ref, *refs):
    out_refs, done = refs[:4], refs[4]
    place = Place()
    sweep = place.sweep(side0_ref.shape[-1])
    saved_refs = (saved0_ref, saved1_ref)

    def saved(side, slot, level, j):
        return saved_refs[slot][side, 0, level, j]

    for side, (edge, halo) in enumerate(((side0_ref, halo0_ref), (side1_ref, halo1_ref))):
        values = wedge(place, sweep, side, edge, halo, saved)
        for slot in range(2):
            for e in range(EDGE):
                done[side, slot, e] = finished(values[slot][e])
    for number, out_ref in enumerate(out_refs):
        slab = place.slab ^ (number % 2)
        side = jnp.where(slab == 1, place.odd, 1 - place.odd)
        out_ref[...] = done[side, number // 2]


def output_kernel(*refs):
    inner_refs, edge_refs, out_ref = refs[:4], refs[4:8], refs[8]
    place = Place()
    half = out_ref.shape[0]
    inner, _, step = inner_refs[0].shape
    for number in range(4):
        lanes = pl.ds(pl.multiple_of((place.chunk ^ number) * step, LANES), step)
        out_ref[pl.ds((1 - place.slab) * EDGE, inner), :, lanes] = inner_refs[number][...]
        for e in range(EDGE):
            out_ref[jnp.where(place.slab == 1, half - 1 - e, e), :, lanes] = edge_refs[number][e]


def on_device(volume, warp_coef, offsets, thresholds):
    frames, slabs = lax.axis_size("tm"), lax.axis_size("space")
    levels = frames.bit_length() - 1
    pairs = slabs // 2
    _, half, rows, length = volume.shape
    planes = 2 * half
    inner = planes - 2 * EDGE
    width = length // 4 + 2 * SPARE
    axes = ("tm", "space")

    def route(frame_bits, slab_bits):
        return [(f * slabs + s, (f ^ frame_bits) * slabs + (s ^ slab_bits)) for f in range(frames) for s in range(slabs)]

    def swap(value, frame_bits, slab_bits=0):
        return lax.ppermute(value, axes, route(frame_bits, slab_bits))

    def spread(pieces):
        return (pieces[0], swap(pieces[1], 0, 1), swap(pieces[2], 2, 0), swap(pieces[3], 2, 1))

    def halo(side0, side1):
        first = [(s, s ^ 2) for s in range(slabs)]
        second = []
        for s in range(slabs):
            pair = s // 2 + 1 if (s // 2) % 2 else s // 2 - 1
            if 0 <= pair < pairs:
                second.append((s, 2 * pair + s % 2))
        return lax.ppermute(side0, "space", first), lax.ppermute(side1, "space", second)

    side_shape = f32(2, EDGE, rows, width)
    inner_shape = f32(2, inner, rows, width)
    saved_shape = f32(2, 2, SWEEPS - 1, 2, rows, width)
    edges_shape = f32(2, 2, EDGE, rows, width)
    level_scratch = pltpu.VMEM((2, planes, rows, width), jnp.float32)
    packed = pltpu.VMEM((BAND, half, length + LANES), jnp.float32)

    received = swap(volume[0], 1)
    early = call(
        early_kernel, [f32(BAND, half, width)] * 4, warp_coef[0, 1], micros=0.8, scratch=[packed],
    )
    early = spread(early)
    pieces = call(
        first_kernel, [f32(half, rows, width)] * 4, volume[0], received, warp_coef, offsets, thresholds,
        spaces={3: SMEM, 4: SMEM}, micros=4.0, scratch=[pltpu.VMEM((half, rows, length + LANES), jnp.float32)],
    )
    pieces, coeff = lax.optimization_barrier((pieces, early))
    late = call(
        late_kernel, [f32(SECTIONS - 2, BAND, half, width)] * 4, warp_coef, offsets, spaces={1: SMEM}, micros=1.5,
        scratch=[packed],
    )
    mine, near, far = pieces[0], swap(pieces[1], 0, 1), swap(pieces[2], 2, 0)
    last, near, far = lax.optimization_barrier((pieces[3], near, far))
    across = swap(last, 2, 1)
    own, saved = call(
        functools.partial(inner_first_kernel, 0), [inner_shape, saved_shape], mine, near,
        scratch=[level_scratch] * 3, micros=3.5,
    )
    across, own = lax.optimization_barrier((across, own))
    side0, side1 = call(start_kernel, [side_shape, side_shape], mine, near, far, across, micros=0.2)
    late, side0 = lax.optimization_barrier((late, side0))
    halo0, halo1 = halo(side0, side1)
    own, saved = call(
        functools.partial(inner_first_kernel, 1), [inner_shape, saved_shape], far, across, own, saved,
        scratch=[level_scratch] * 3, micros=3.5, aliases={2: 0, 3: 1},
    )
    late = spread(late)
    table = None
    for section in range(1, SECTIONS):
        bit = section % levels
        corners = [(0,)] if section == 1 else [(section - 2, 0)]
        edges, *shift = call(
            functools.partial(wedge_kernel, corners),
            [edges_shape] + [jax.ShapeDtypeStruct((len(corners), 2, 2), jnp.int32)] * bool(corners),
            side0, side1, halo0, halo1, saved, *((mine, near, far, across) if section == 1 else coeff),
            smem_outs=(1,), micros=2.4,
        )
        table = shift[0] if shift else table
        partner, partner_edges = own, edges
        if bit != 1:
            partner, partner_edges = lax.optimization_barrier((own, swap(edges, 1 << bit)))
            partner = swap(partner, 1 << bit)
        side0, side1 = call(
            functools.partial(haar_kernel, section, bit), [side_shape, side_shape],
            edges, partner_edges, table, thresholds, *coeff, spaces={2: SMEM, 3: SMEM}, micros=1.1,
            scratch=[pltpu.VMEM((2, 2, EDGE, rows, width), jnp.float32)],
        )
        used = table, thresholds, *coeff
        if section == 1:
            late, own = lax.optimization_barrier((late, own))
            partner = own
            coeff = late
        halo0, halo1 = halo(side0, side1)
        if section == SECTIONS - 1:
            break
        own, saved = call(
            functools.partial(inner_kernel, section, bit), [inner_shape, saved_shape],
            own, partner, side0, side1, *used,
            spaces={4: SMEM, 5: SMEM}, scratch=[level_scratch] * 3, micros=8.0,
        )
    piece_shape = f32(half - EDGE, rows, length // 4)
    edge_shape = f32(EDGE, rows, length // 4)
    slot_saved = f32(2, 1, SWEEPS - 1, 2, rows, width)

    def last_inner(slot):
        return call(
            functools.partial(inner_last_kernel, section, bit, slot), [piece_shape, piece_shape, slot_saved],
            own, partner, side0, side1, *used, spaces={4: SMEM, 5: SMEM}, micros=4.2,
            scratch=[level_scratch] * 3 + [pltpu.VMEM((inner, rows, length // 4), jnp.float32)],
        )

    far, across, saved1 = last_inner(1)
    across = swap(across, 2, 1)
    mine, near, saved0 = last_inner(0)
    across, halo0 = lax.optimization_barrier((across, halo0))
    inners = (mine, swap(near, 0, 1), swap(far, 2, 0), across)
    edges = call(
        wedge_last_kernel, [edge_shape] * 4, side0, side1, halo0, halo1, saved0, saved1, micros=2.5,
        scratch=[pltpu.VMEM((2, 2, EDGE, rows, length // 4), jnp.float32)],
    )
    (out,) = call(output_kernel, [f32(half, rows, length)], *inners, *spread(edges), micros=1.0)
    return out[None]


def solution(mesh):
    return jax.shard_map(
        on_device,
        mesh=mesh,
        in_specs=(
            P("tm", "space", None, None),
            P("tm", None, None, "space", None),
            P("tm", "space", None),
            P(),
        ),
        out_specs=P("tm", "space", None, None),
        check_vma=False,
    )
```
